32 devices in a mesh: dp: 8 (over z, y), fsdp: 4 (over x, core).
Axes of the slice: x: 2, y: 2, z: 4, core: 2. Of those that a mesh axis runs over, the one named last changes fastest.
Arguments:
- tokens: bfloat16 [16, 256, 2048], P(None, ('dp', 'fsdp')), may hold values from -6 to 6
- cotangent: bfloat16 [16, 256, 2048], P(None, ('dp', 'fsdp')), may hold values from -6 to 6
- lengths: int32 [16], replicated, may hold values from 1 to 256, 3072 in all
- order: int32 [16], replicated, may hold values from 0 to 15, each once
- routes: int32 [16, 256, 4], replicated, may hold values from 0 to 7, all different within a row
- norm_attn: bfloat16 [2048], P(('dp', 'fsdp')), may hold values from 0.5 to 1.5
- q_weight: bfloat16 [2048, 2048], P(('dp', 'fsdp')), may hold values from -0.125 to 0.125
- k_weight: bfloat16 [2048, 2048], P(('dp', 'fsdp')), may hold values from -0.125 to 0.125
- v_weight: bfloat16 [2048, 2048], P(('dp', 'fsdp')), may hold values from -0.125 to 0.125
- q_bias: bfloat16 [2048], P(('dp', 'fsdp')), may hold values from -3 to 3
- k_bias: bfloat16 [2048], P(('dp', 'fsdp')), may hold values from -3 to 3
- v_bias: bfloat16 [2048], P(('dp', 'fsdp')), may hold values from -3 to 3
- o_weight: bfloat16 [2048, 2048], P(('dp', 'fsdp')), may hold values from -0.75 to 0.75
- norm_moe: bfloat16 [2048], P(('dp', 'fsdp')), may hold values from 0.5 to 1.5
- router: bfloat16 [2048, 8], P(('dp', 'fsdp')), may hold values from -0.0625 to 0.0625
- shared_gate: bfloat16 [2048], P(('dp', 'fsdp')), may hold values from -0.125 to 0.125
- shared_gate_up: bfloat16 [2048, 11264], P(('dp', 'fsdp')), may hold values from -0.125 to 0.125
- shared_down: bfloat16 [5632, 2048], P(('dp', 'fsdp')), may hold values from -0.15625 to 0.15625
- expert_gate_up: bfloat16 [8, 2048, 2816], P('dp', 'fsdp'), may hold values from -0.125 to 0.125
- expert_down: bfloat16 [8, 1408, 2048], P('dp', 'fsdp'), may hold values from -0.875 to 0.875
Outputs:
- mixed: bfloat16 [16, 256, 2048], P(None, ('dp', 'fsdp'))
- grad_tokens: bfloat16 [16, 256, 2048], P(None, ('dp', 'fsdp'))
- grad_norm_attn: float32 [2048], P(('dp', 'fsdp'))
- grad_q_weight: float32 [2048, 2048], P(('dp', 'fsdp'))
- grad_k_weight: float32 [2048, 2048], P(('dp', 'fsdp'))
- grad_v_weight: float32 [2048, 2048], P(('dp', 'fsdp'))
- grad_q_bias: float32 [2048], P(('dp', 'fsdp'))
- grad_k_bias: float32 [2048], P(('dp', 'fsdp'))
- grad_v_bias: float32 [2048], P(('dp', 'fsdp'))
- grad_o_weight: float32 [2048, 2048], P(('dp', 'fsdp'))
- grad_norm_moe: float32 [2048], P(('dp', 'fsdp'))
- grad_router: float32 [2048, 8], P(('dp', 'fsdp'))
- grad_shared_gate: float32 [2048], P(('dp', 'fsdp'))
- grad_shared_gate_up: float32 [2048, 11264], P(('dp', 'fsdp'))
- grad_shared_down: float32 [5632, 2048], P(('dp', 'fsdp'))
- grad_expert_gate_up: float32 [8, 2048, 2816], P('dp', 'fsdp')
- grad_expert_down: float32 [8, 1408, 2048], P('dp', 'fsdp')
The draws below stay inside these ranges and needn't reach their ends.
Inputs may be any that keep to these rules, and one draw needn't show every extreme that they name: `lengths`: some sequence is exactly 256 long. `order`: each sequence number once. `routes`: the 4 experts of a token differ.
All inputs are finite; a program needn't handle non-finite values.
Results may differ from the reference program's by a relative error of at most 0.03.
Values may be sent and summed in bfloat16 or wider, within the bound.
No kernel may reach another device: no remote copies, remote signals or barrier semaphores. Data moves between devices by JAX's collectives and lax.ppermute only.
A program may use at most 448 MiB of HBM per device.

```python
import math
import jax
import jax.numpy as jnp
import numpy as np
from jax import lax

D = 2048
HEADS = 16
HEAD = 128
EFF = 1408
SFF = 5632
TOP = 4
MAXLEN = 256
SEQ_GRP = 2
NSEQ = 16
PDEV = 8
EXPERTS = 8
CAP = 80
N_DP = 8
N_FSDP = 4


def level_of(stream_key, shape, cuts, low, top_value):
    gain, own = 1.0, jax.random.fold_in(stream_key, 6)
    for position, blocks in cuts:
        heights = jnp.exp(jax.random.uniform(jax.random.fold_in(own, position), (blocks,), jnp.float32, low / len(cuts), top_value / len(cuts)))
        gain = gain * jnp.repeat(heights, shape[position] // blocks).reshape([-1 if axis == position else 1 for axis in range(len(shape))])
    return gain


def distinct(key, rows, amount, top, lift):
    sequence = jax.random.permutation(jax.random.fold_in(key, 1), amount)
    boost = sequence
    for power in range(3):
        boost = boost * boost // amount
    boost = boost * lift // amount
    tickets = jax.random.randint(jax.random.fold_in(key, 2), (rows, amount), 0, 4096) + boost
    fixed_rows = jax.random.permutation(jax.random.fold_in(key, 3), rows)[jnp.arange(amount) % rows]
    tickets = jnp.where(jnp.arange(rows)[:, None] == fixed_rows[None, :], 1 << 14, tickets)
    merit = tickets * amount + jnp.arange(amount)
    return lax.top_k(merit.astype(jnp.int32), top)[1].astype(jnp.int32)


def profile(count, total, bound, skew):
    weights = [(1 << 20) // math.isqrt(standing ** skew) + 1 for standing in range(2, count + 1)]
    rest, given = total - bound - (count - 1), [1] * (count - 1)
    while rest > 0:
        free = [i for i in range(count - 1) if given[i] < bound]
        pool, left = sum([weights[i] for i in free]), rest
        for i in free:
            addition = min(bound - given[i], max(1, left * weights[i] // pool), rest)
            given[i] = given[i] + addition
            rest = rest - addition
    return np.array([bound] + given)


def ragged(own_key, number_of, total, bound, lean):
    if number_of == 2:
        one = jax.random.randint(own_key, (), max(1, total - bound), min(bound, total - 1) + 1)
        return jnp.stack([one, total - one])
    sizes = jnp.asarray(profile(number_of, total, bound, lean), jnp.int32)
    pairs = (number_of - 1) // 2
    giver, sink = sizes[1:1 + 2 * pairs:2], sizes[2:2 + 2 * pairs:2]
    margin = jnp.minimum(giver - 1, bound - sink)
    passed = jax.random.randint(jax.random.fold_in(own_key, 1), (pairs,), 0, 1 << 20) % (margin + 1)
    sizes = sizes.at[1:1 + 2 * pairs:2].set(giver - passed).at[2:2 + 2 * pairs:2].set(sink + passed)
    return sizes[jax.random.permutation(jax.random.fold_in(own_key, 2), number_of)]


def bell_draw(rng, dims, width, reach, pieces=(), kind=jnp.bfloat16):
    entries = jax.random.normal(rng, dims, jnp.float32) * width
    if len(pieces) > 0:
        entries = level_of(rng, dims, pieces, -0.22, 0.18) * entries
    return jnp.clip(entries, min=-reach, max=reach).astype(kind)


def setup_inputs(seed: int = 0) -> dict:
    seeds = jax.random.split(jax.random.key(seed), 21)
    return {
        "tokens": bell_draw(seeds[0], (NSEQ, MAXLEN, D), 1.0, 6.0, ((1, 32),)),
        "cotangent": bell_draw(seeds[1], (NSEQ, MAXLEN, D), 1.0, 6.0, ((1, 32),)),
        "lengths": ragged(seeds[2], NSEQ, NSEQ * MAXLEN * 3 // 4, MAXLEN, 1).astype(jnp.int32),
        "order": jax.random.permutation(seeds[3], NSEQ).astype(jnp.int32),
        "routes": distinct(seeds[4], NSEQ * MAXLEN, EXPERTS, TOP, 8192).reshape((NSEQ, MAXLEN, TOP)),
        "norm_attn": jnp.clip(1.0 + 0.1 * jax.random.normal(seeds[5], (D,), jnp.float32), 0.5, 1.5).astype(jnp.bfloat16),
        "q_weight": bell_draw(seeds[6], (D, D), D ** -0.5, 0.125, ((0, 32),)),
        "k_weight": bell_draw(seeds[7], (D, D), D ** -0.5, 0.125, ((0, 32),)),
        "v_weight": bell_draw(seeds[8], (D, D), D ** -0.5, 0.125, ((0, 32),)),
        "q_bias": bell_draw(seeds[9], (D,), 0.5, 3.0, ((0, 32),)),
        "k_bias": bell_draw(seeds[10], (D,), 0.5, 3.0, ((0, 32),)),
        "v_bias": bell_draw(seeds[11], (D,), 0.5, 3.0, ((0, 32),)),
        "o_weight": bell_draw(seeds[12], (D, D), (D // 32) ** -0.5, 0.75, ((0, 32),)),
        "norm_moe": jnp.clip(1.0 + 0.1 * jax.random.normal(seeds[13], (D,), jnp.float32), 0.5, 1.5).astype(jnp.bfloat16),
        "router": bell_draw(seeds[14], (D, EXPERTS), (4 * D) ** -0.5, 0.0625, ((0, 32),)),
        "shared_gate": bell_draw(seeds[15], (D,), D ** -0.5, 0.125, ((0, 32),)),
        "shared_gate_up": bell_draw(seeds[16], (D, 2 * SFF), D ** -0.5, 0.125, ((0, 32),)),
        "shared_down": bell_draw(seeds[17], (SFF, D), (SFF // 4) ** -0.5, 0.15625, ((0, 32),)),
        "expert_gate_up": bell_draw(seeds[18], (EXPERTS, D, 2 * EFF), D ** -0.5, 0.125, ((0, 8), (1, 4))),
        "expert_down": bell_draw(seeds[19], (EXPERTS, EFF, D), (EFF // 32) ** -0.5, 0.875, ((0, 8), (1, 4))),
    }


@jax.custom_vjp
def low(v):
    return lax.optimization_barrier(v.astype(jnp.bfloat16)).astype(jnp.float32)

@jax.custom_vjp
def low_back(v):
    return v

def low_keep(v):
    return (low(v), None)

def low_pass(kept, grad):
    return (grad,)

def back_keep(v):
    return (v, None)

def back_low(kept, grad):
    return (low(grad),)
low.defvjp(low_keep, low_pass)
low_back.defvjp(back_keep, back_low)
epsilon = 1e-06
rope_base = 1000000.0
negative = -1e+30

def product(matrix, operand):
    return jnp.dot(matrix, operand, precision=lax.Precision.HIGHEST)

def rotary_tables(positions):
    freq_index = jnp.arange(HEAD // 2).astype(jnp.float32)
    inverse = jnp.exp(freq_index * (-2.0 * math.log(rope_base) / HEAD))
    angles = positions.astype(jnp.float32)[:, None] * inverse[None, :]
    cosine = jnp.concatenate([jnp.cos(angles), jnp.cos(angles)], axis=-1)
    sine_table = jnp.concatenate([jnp.sin(angles), jnp.sin(angles)], axis=-1)
    return (cosine, sine_table)

def rotate(values, cosine, sine_table):
    half_width = values.shape[-1] // 2
    turned = jnp.concatenate([-values[..., half_width:], values[..., :half_width]], axis=-1)
    return values * cosine[:, None, :] + turned * sine_table[:, None, :]

def rms_scale(values, gain_vector):
    return values * lax.rsqrt(lax.optimization_barrier(jnp.mean(values * values, axis=-1, keepdims=True)) + epsilon) * gain_vector

def swiglu(joined, hidden_width):
    return jax.nn.silu(joined[..., :hidden_width]) * joined[..., hidden_width:]

def group_layer(items, params):
    block, seq_lengths, seq_routes = items
    norm_attn, q_weight, k_weight, v_weight, q_bias, k_bias, v_bias, o_weight, norm_moe, router, shared_gate, shared_gate_up, shared_down, expert_gate_up, expert_down = params
    token_count = SEQ_GRP * MAXLEN
    row_block = block.reshape(token_count, D)
    positions = jnp.arange(MAXLEN, dtype=jnp.int32)
    live_int = (positions[None, :] < seq_lengths[:, None]).astype(jnp.int32).reshape(token_count, 1)
    live_rows = live_int.astype(jnp.float32)
    normed_one = low(rms_scale(row_block, norm_attn))
    cosine, sine_table = rotary_tables(positions)
    shape_four = (SEQ_GRP, MAXLEN, HEADS, HEAD)
    queries = low(rotate(low_back(product(normed_one, q_weight) + q_bias).reshape(shape_four), cosine, sine_table))
    keys = low(rotate(low_back(product(normed_one, k_weight) + k_bias).reshape(shape_four), cosine, sine_table))
    values = low(low_back(product(normed_one, v_weight) + v_bias)).reshape(shape_four)
    scores = low_back(jnp.einsum('sqhd,skhd->shqk', queries, keys, precision=lax.Precision.HIGHEST) * HEAD ** (-0.5))
    causal = positions[None, :] <= positions[:, None]
    scores = jnp.where(causal[None, None], scores, negative)
    weights = jax.nn.softmax(scores, axis=-1)
    combined = jnp.einsum('shqk,skhd->sqhd', low(weights), values, precision=lax.Precision.HIGHEST).reshape(token_count, D)
    attended = low(low_back(combined))
    residual = row_block + live_rows * low_back(product(attended, o_weight))
    normed_two = low(rms_scale(residual, norm_moe))
    logits = low_back(product(normed_two, router))
    router_probs = jax.nn.softmax(logits, axis=-1)
    flat_routes = seq_routes.reshape(token_count, TOP)
    gates = jnp.take_along_axis(router_probs, flat_routes, axis=1)
    chosen = (flat_routes[:, :, None] == jnp.arange(EXPERTS, dtype=jnp.int32)[None, None, :]).astype(jnp.int32)
    marks = lax.optimization_barrier(jnp.sum(chosen, axis=1)) * live_int
    marks = marks.reshape(SEQ_GRP, N_DP, N_FSDP, PDEV, EXPERTS).transpose(2, 0, 1, 3, 4).reshape(N_FSDP, -1, EXPERTS)
    before = jnp.cumsum(marks, axis=1) - marks
    before = before.reshape(N_FSDP, SEQ_GRP, N_DP, PDEV, EXPERTS).transpose(1, 2, 0, 3, 4).reshape(token_count, EXPERTS)
    places = jnp.take_along_axis(before, flat_routes, axis=1)
    kept_bool = (live_int > 0) & (places < CAP)
    owner = positions // PDEV % N_FSDP
    owners = jnp.tile(owner, SEQ_GRP)[:, None]
    dummy_slot = N_FSDP * EXPERTS * CAP
    slots = jnp.where(kept_bool, (owners * EXPERTS + flat_routes) * CAP + places, dummy_slot).reshape(-1)
    pair_rows = low_back(jnp.broadcast_to(normed_two[:, None, :], (token_count, TOP, D))).reshape(-1, D)
    buffer = jax.ops.segment_sum(pair_rows, slots, num_segments=dummy_slot + 1)[:dummy_slot]
    buffer = buffer.reshape(N_FSDP, EXPERTS, CAP, D).transpose(1, 0, 2, 3).reshape(EXPERTS, N_FSDP * CAP, D)
    joined = low_back(jnp.einsum('end,edf->enf', buffer, expert_gate_up, precision=lax.Precision.HIGHEST))
    hidden = low(swiglu(joined, EFF))
    produced = low(low_back(jnp.einsum('enf,efd->end', hidden, expert_down, precision=lax.Precision.HIGHEST)))
    produced = produced.reshape(EXPERTS, N_FSDP, CAP, D).transpose(1, 0, 2, 3).reshape(dummy_slot, D)
    produced = jnp.concatenate([produced, jnp.zeros((1, D), produced.dtype)], axis=0)
    returned = jnp.take(produced, slots, axis=0).reshape(token_count, TOP, D)
    kept_float = kept_bool.astype(jnp.float32)
    routed = lax.optimization_barrier(jnp.sum((gates * kept_float)[:, :, None] * returned, axis=1))
    shared_joined = low_back(product(normed_two, shared_gate_up))
    shared_hidden = low(swiglu(shared_joined, SFF))
    shared_out = low_back(product(shared_hidden, shared_down))
    shared_weight = jax.nn.sigmoid(product(normed_two, shared_gate))
    total = residual + live_rows * (shared_weight[:, None] * shared_out + routed)
    return total.reshape(SEQ_GRP, MAXLEN, D)

def forward(inputs, params, lengths, order, routes):
    grouped = jnp.take(inputs, order, axis=0).reshape(N_DP, SEQ_GRP, MAXLEN, D)
    group_lengths = jnp.take(lengths, order).reshape(N_DP, SEQ_GRP)
    group_routes = jnp.take(routes, order, axis=0).reshape(N_DP, SEQ_GRP, MAXLEN, TOP)
    layer_step = jax.checkpoint(group_layer)

    def scan_step(carry, items):
        return (carry, layer_step(items, params))
    final_carry, results = lax.scan(scan_step, jnp.zeros((), jnp.float32), (grouped, group_lengths, group_routes))
    return jnp.zeros_like(inputs).at[order].set(results.reshape(NSEQ, MAXLEN, D))

def reference(tokens, cotangent, lengths, order, routes, norm_attn, q_weight, k_weight, v_weight, q_bias, k_bias, v_bias, o_weight, norm_moe, router, shared_gate, shared_gate_up, shared_down, expert_gate_up, expert_down):
    initials = (norm_attn, q_weight, k_weight, v_weight, q_bias, k_bias, v_bias, o_weight, norm_moe, router, shared_gate, shared_gate_up, shared_down, expert_gate_up, expert_down)
    params = tuple((weight.astype(jnp.float32) for weight in initials))
    inputs = tokens.astype(jnp.float32)

    def whole_layer(inputs_arg, params_arg):
        return forward(inputs_arg, params_arg, lengths, order, routes)
    layer_out, pullback = jax.vjp(whole_layer, inputs, params)
    grad_inputs, gradients = pullback(cotangent.astype(jnp.float32))
    return (layer_out.astype(jnp.bfloat16), grad_inputs.astype(jnp.bfloat16), gradients[0], gradients[1], gradients[2], gradients[3], gradients[4], gradients[5], gradients[6], gradients[7], gradients[8], gradients[9], gradients[10], gradients[11], gradients[12], gradients[13], gradients[14])
```

```python
import math

import jax
import jax.numpy as jnp
import numpy as np
from jax import lax
from jax.sharding import Mesh
from jax.sharding import PartitionSpec as P

HEAD = 128
TOP = 4
AXES = ("dp", "x", "core")
CHIPS = ("dp", "x")
SPLITS = (48, 40, 40)
LOW = (1, 2, 3)

epsilon = 1e-06
rope_base = 1000000.0
negative = -1e30
F32 = jnp.float32
BF16 = jnp.bfloat16


def mm(a, b):
    return lax.dot_general(a, b, (((1,), (0,)), ((), ())), preferred_element_type=F32)


def mm_tn(a, b):
    return lax.dot_general(a, b, (((0,), (0,)), ((), ())), preferred_element_type=F32)


def mm_nt(a, b):
    return lax.dot_general(a, b, (((1,), (1,)), ((), ())), preferred_element_type=F32)


def devices():
    return lax.axis_size("dp") * 4


def permute(value, pairs):
    return lax.ppermute(value, AXES, pairs)


def swap(value, bit):
    return permute(value, [(i, i ^ (1 << bit)) for i in range(devices())])


def gather_bits(value, bits):
    for bit in bits:
        value = jnp.stack([value, swap(value, bit)])
    return value


def add_low(a, b):
    return (a.astype(F32) + b.astype(F32)).astype(BF16)


def scatter_bits(value, bits):
    for bit in reversed(bits):
        value = add_low(value[0], swap(value[1], bit))
    return value


def pieces(rows):
    start = 0
    found = []
    for count in SPLITS:
        found.append(lax.slice_in_dim(rows, start, start + count, axis=-2))
        start += count
    return found


def rotations(high):
    return [high + (3, 1, 2), high + (1, 2, 3), high + (2, 3, 1)]


def to_order(value, bits, wanted):
    have = tuple(reversed(bits))
    lead = [have.index(bit) for bit in wanted]
    rest = list(range(len(bits), value.ndim))
    return value.transpose(lead + rest)


def relative(bits):
    found = np.zeros((1,), np.int64)
    for bit in bits:
        found = np.concatenate([found, found ^ (1 << bit)])
    return found


def by_bit(mine, theirs, flag, axis):
    low = jnp.where(flag == 0, mine, theirs)
    high = jnp.where(flag == 0, theirs, mine)
    return jnp.stack([low, high], axis=axis)


def xor_order(value, number):
    count = value.shape[0]
    return jnp.stack(
        [lax.dynamic_index_in_dim(value, number ^ k, 0, keepdims=False) for k in range(count)]
    )


def deal(value, part, high):
    parts = 2 << len(high)
    shape = value.shape
    value = xor_order(value.reshape((parts, shape[0] // parts) + shape[1:]), part)
    value = value.reshape((2,) * (len(high) + 1) + value.shape[1:])
    left = len(high) + 1
    for bit in tuple(reversed(high)) + (0,):
        left -= 1
        value = jnp.stack([value[0], swap(value[1], bit)], axis=left)
    return value


def undeal(value, part, high):
    done = 0
    for bit in (0,) + tuple(high):
        keep = lax.index_in_dim(value, 0, done, keepdims=False)
        give = lax.index_in_dim(value, 1, done, keepdims=False)
        value = jnp.stack([keep, swap(give, bit)])
        done += 1
    shape = value.shape[done:]
    value = xor_order(value.reshape((1 << done,) + shape), part)
    return value.reshape((value.shape[0] * shape[0],) + shape[1:])


def rotary_tables(positions):
    freq_index = jnp.arange(HEAD // 2).astype(F32)
    inverse = jnp.exp(freq_index * (-2.0 * math.log(rope_base) / HEAD))
    angles = positions.astype(F32)[:, None] * inverse[None, :]
    cosine = jnp.concatenate([jnp.cos(angles), jnp.cos(angles)], axis=-1)
    sine_table = jnp.concatenate([jnp.sin(angles), jnp.sin(angles)], axis=-1)
    return (cosine, sine_table)


def rotate(values, cosine, sine_table):
    half_width = HEAD // 2
    turned = jnp.concatenate([-values[..., half_width:], values[..., :half_width]], axis=-1)
    return values * cosine + turned * sine_table


def rotate_back(grads_in, cosine, sine_table):
    half_width = HEAD // 2
    scaled = grads_in * sine_table
    turned = jnp.concatenate([scaled[..., half_width:], -scaled[..., :half_width]], axis=-1)
    return grads_in * cosine + turned


def normalize(values):
    factor = lax.rsqrt(jnp.mean(values * values, axis=-1, keepdims=True) + epsilon)
    return (values * factor, factor)


def norm_back(grad_normed, normal, factor, gain_vector):
    scaled = grad_normed * gain_vector
    grad_input = factor * (scaled - normal * jnp.mean(scaled * normal, axis=-1, keepdims=True))
    return (grad_input, jnp.sum(grad_normed * normal, axis=0))


def on_device(
    tokens,
    cotangent,
    lengths,
    order,
    routes,
    norm_attn,
    q_weight,
    k_weight,
    v_weight,
    q_bias,
    k_bias,
    v_bias,
    o_weight,
    norm_moe,
    router,
    shared_gate,
    shared_gate_up,
    shared_down,
    expert_gate_up,
    expert_down,
):
    total = devices()
    chips = total // 2
    bit_count = total.bit_length() - 1
    high = tuple(range(4, bit_count))
    me = lax.axis_index(AXES)
    core = me & 1
    x_bit = (me >> 1) & 1
    pair = (me >> 1) & 7
    upper = me >> 4
    uppers = total // 16
    parts = 2 * uppers
    part = upper * 2 + core
    my_expert = me >> 2
    sequences, piece, width = tokens.shape
    experts = router.shape[1]
    rows = sequences * piece
    length = total * piece
    own_seq = sequences // parts
    depth = q_weight.shape[0]
    heads = width // HEAD
    shared_width = shared_down.shape[0] * total // chips
    expert_width = expert_down.shape[1] * 2
    hidden_width = shared_width + expert_width
    padded = -(-(hidden_width + experts + 1) // 128) * 128
    groups = total // 4
    per_group = sequences // groups
    group_rows = per_group * groups * piece
    capacity = (5 * group_rows * TOP + 4 * experts - 1) // (4 * experts)
    score_scale = HEAD ** (-0.5)
    low_orders = rotations(())
    full_orders = rotations(tuple(reversed(high)))

    small = jnp.concatenate(
        [
            jnp.stack([norm_attn, q_bias, k_bias, v_bias, norm_moe, shared_gate]),
            router.T,
            jnp.zeros((2, depth), BF16),
        ]
    )
    small = lax.all_gather(small, AXES, axis=0)
    small = small.transpose(1, 0, 2).reshape(small.shape[1], width)
    gain_attn = small[0].astype(F32)
    gain_moe = small[4].astype(F32)
    biases = lax.dynamic_slice_in_dim(small[1:4].reshape(3, heads // 2, 2, HEAD), pair, 1, axis=1)
    biases = biases[:, 0].transpose(1, 0, 2).astype(F32)

    token_parts = [
        gather_bits(value, bits)
        for value, bits in zip(
            pieces(deal(tokens, part, high).reshape(rows, width)), low_orders, strict=True
        )
    ]

    stacked = jnp.stack([q_weight, k_weight, v_weight], axis=1)
    by_head = stacked.reshape(depth, 3, 16, HEAD).transpose(2, 0, 1, 3).reshape(16, depth, 3 * HEAD)
    by_head = jnp.broadcast_to(by_head[None], (uppers,) + by_head.shape)
    my_head = lax.all_to_all(
        by_head.reshape(total, depth, 3 * HEAD), AXES, split_axis=0, concat_axis=0, tiled=True
    ).reshape(width, 3 * HEAD)
    qkv_weight = by_bit(my_head, swap(my_head, 0), core, 1).reshape(width, 6 * HEAD)

    o_places = []
    for k in range(uppers):
        o_places.append(
            [
                (
                    i,
                    (((i % parts >> 1) ^ k) << 4) | ((i // parts) << 1) | (i & 1),
                )
                for i in range(total)
            ]
        )
    o_rows = xor_order(jnp.stack([permute(o_weight, places) for places in o_places]), upper)
    o_rows = by_bit(o_rows, swap(o_rows, 0), core, 1).reshape(2 * HEAD, width)

    own_positions = me * piece + jnp.arange(piece, dtype=jnp.int32)
    live_own = (own_positions[None, :] < lengths[:, None]).astype(F32)[:, :, None]
    grad_out = cotangent.astype(F32)
    branch_own = (live_own * grad_out).astype(BF16).reshape(rows, width)
    branch_parts = [
        gather_bits(value, bits)
        for value, bits in zip(pieces(branch_own), full_orders, strict=True)
    ]

    shared_pieces = (
        shared_gate_up.reshape(depth, 2, chips, shared_width)
        .transpose(2, 0, 1, 3)
        .reshape(chips, depth, 2 * shared_width)
    )
    shared_in = lax.all_to_all(shared_pieces, CHIPS, split_axis=0, concat_axis=0, tiled=True)
    shared_in = by_bit(shared_in, swap(shared_in, 0), core, 1).reshape(width, 2, shared_width)
    expert_rows = expert_gate_up.shape[1]
    expert_halves = expert_gate_up[0].reshape(expert_rows, 2, 2, expert_width)
    keep_half = jnp.where(x_bit == 0, expert_halves[:, :, 0], expert_halves[:, :, 1])
    give_half = jnp.where(x_bit == 0, expert_halves[:, :, 1], expert_halves[:, :, 0])
    expert_in = by_bit(keep_half, swap(give_half, 1), x_bit, 0)
    expert_in = by_bit(expert_in, swap(expert_in, 0), core, 1).reshape(width, 2, expert_width)
    spare = padded - hidden_width
    extra = jnp.concatenate(
        [small[6 : 6 + experts], small[5:6], jnp.zeros((spare - experts - 1, width), BF16)]
    ).T
    gate_weight = jnp.concatenate([shared_in[:, 0], expert_in[:, 0], extra], axis=1)
    up_weight = jnp.concatenate(
        [shared_in[:, 1], expert_in[:, 1], jnp.zeros((width, spare), BF16)], axis=1
    )
    shared_out_rows = by_bit(shared_down, swap(shared_down, 0), core, 0).reshape(-1, width)
    expert_out_rows = by_bit(expert_down[0], swap(expert_down[0], 0), core, 0).reshape(-1, width)
    down_weight = jnp.concatenate(
        [shared_out_rows, expert_out_rows, jnp.zeros((spare, width), BF16)]
    )

    all_positions = jnp.arange(length, dtype=jnp.int32)
    named = jnp.any(routes == my_expert, axis=-1) & (all_positions[None, :] < lengths[:, None])
    dealt = (
        jnp.take(named, order, axis=0)
        .reshape(groups, per_group, length // (4 * piece), 4, piece)
        .transpose(0, 3, 1, 2, 4)
        .reshape(groups * 4, group_rows)
        .astype(BF16)
    )
    index = jnp.arange(group_rows, dtype=jnp.int32)
    before = mm(dealt, (index[:, None] < index[None, :]).astype(BF16))
    kept = (
        jnp.where(before < capacity, dealt.astype(F32), 0.0)
        .reshape(groups, 4, per_group, length // (4 * piece), piece)
        .transpose(0, 2, 3, 1, 4)
        .reshape(sequences, length)
    )
    seq_index = jnp.arange(sequences, dtype=jnp.int32)
    place_of = jnp.sum(
        jnp.where(order[None, :] == seq_index[:, None], seq_index[None, :], 0), axis=1
    )
    kept = (
        jnp.take(kept, place_of, axis=0)
        .reshape(sequences, total, piece)
        .transpose(1, 0, 2)
        .reshape(total, rows)
    )

    wanted = (3, 2, 1)
    normed_parts = []
    projected = []
    for value, bits in zip(token_parts, low_orders, strict=True):
        flat = value.reshape(-1, width).astype(F32)
        normed = (normalize(flat)[0] * gain_attn).astype(BF16)
        normed_parts.append(normed)
        out = mm(normed, qkv_weight).reshape(value.shape[:-1] + (6 * HEAD,))
        projected.append(to_order(out, bits, wanted))
    shape_rows = (8, parts, own_seq, piece, 2, 3, HEAD)
    joined = jnp.concatenate(projected, axis=-2).reshape(shape_rows)
    joined = joined + biases
    joined = joined.transpose(5, 2, 4, 0, 1, 3, 6).reshape(3, own_seq, 2, length, HEAD)
    source = relative(tuple(reversed(high)) + (0,))
    low_relative = relative(LOW)
    rel = (low_relative[:, None] ^ source[None, :]).reshape(-1)
    positions = (
        (me ^ jnp.asarray(rel, jnp.int32))[:, None] * piece
        + jnp.arange(piece, dtype=jnp.int32)[None, :]
    ).reshape(-1)
    causal = positions[None, :] <= positions[:, None]
    cosine, sine_table = rotary_tables(positions)
    queries = rotate(joined[0], cosine, sine_table).astype(BF16)
    keys = rotate(joined[1], cosine, sine_table).astype(BF16)
    values = joined[2].astype(BF16)
    scores = (
        jnp.einsum("shqd,shkd->shqk", queries, keys, preferred_element_type=F32) * score_scale
    )
    masked = jnp.where(causal[None, None], scores, negative)
    top_score = jnp.max(masked, axis=-1, keepdims=True)
    log_total = top_score + jnp.log(jnp.sum(jnp.exp(masked - top_score), axis=-1, keepdims=True))
    probs = jnp.exp(masked - log_total).astype(BF16)
    attended = jnp.einsum("shqk,shkd->shqd", probs, values, preferred_element_type=F32)

    def to_parts(value):
        columns = value.shape[0]
        value = value.reshape(columns, own_seq, 2, 8, parts, piece, HEAD)
        value = value.transpose(3, 4, 1, 5, 2, 0, 6).reshape(2, 2, 2, rows, 2 * columns * HEAD)
        return [
            to_order(part_rows, (1, 2, 3), tuple(reversed(bits))).reshape(
                8 * part_rows.shape[-2], -1
            )
            for part_rows, bits in zip(pieces(value), low_orders, strict=True)
        ]

    def reduce_low(parts_in):
        found = [
            scatter_bits(value.astype(BF16).reshape(2, 2, 2, -1, width), bits)
            for value, bits in zip(parts_in, low_orders, strict=True)
        ]
        found = jnp.concatenate(found).reshape(
            (2,) * (1 + len(high)) + (own_seq, piece, width)
        )
        return undeal(found, part, high)

    attended_parts = to_parts(attended.astype(BF16)[None])
    attn_out = reduce_low([mm(value, o_rows) for value in attended_parts])
    inputs = tokens.astype(F32)
    residual = (inputs + live_own * attn_out.astype(F32)).reshape(rows, width)
    normal_two, factor_two = normalize(residual)
    normed_own = (normal_two * gain_moe).astype(BF16)

    column = jnp.arange(padded, dtype=jnp.int32)[None, :]
    is_shared = column < shared_width
    expert_column = jnp.arange(experts, dtype=jnp.int32)[None, :]
    one_expert = (expert_column == my_expert).astype(F32)
    out_parts = []
    grad_parts = []
    grad_gate = grad_up = grad_down = 0.0
    for normed, branch, bits, start in zip(
        pieces(normed_own), branch_parts, full_orders, (0, 48, 88), strict=True
    ):
        count = normed.shape[0]
        everyone = gather_bits(normed, bits)
        lead = everyone.shape[:-1]
        everyone = everyone.reshape(-1, width)
        branch = branch.reshape(-1, width)
        mask = jnp.take(
            kept[:, start : start + count], me ^ jnp.asarray(relative(bits), jnp.int32), axis=0
        ).reshape(-1, 1)
        gate = mm(everyone, gate_weight)
        up = mm(everyone, up_weight)
        back = mm_nt(branch, down_weight)
        logits = gate[:, hidden_width : hidden_width + experts]
        router_probs = jax.nn.softmax(logits, axis=-1)
        shared_weight = jax.nn.sigmoid(
            gate[:, hidden_width + experts : hidden_width + experts + 1]
        )
        my_prob = jnp.sum(router_probs * one_expert, axis=1, keepdims=True)
        weight = jnp.where(is_shared, shared_weight, my_prob * mask)
        sigmoid_gate = jax.nn.sigmoid(gate)
        hidden = gate * sigmoid_gate * up
        hidden_low = (hidden * weight).astype(BF16)
        grad_hidden = back * weight
        along = hidden * back
        shared_along = jnp.sum(jnp.where(is_shared, along, 0.0), axis=1, keepdims=True)
        expert_along = jnp.sum(jnp.where(is_shared, 0.0, along), axis=1, keepdims=True) * mask
        logit_grad = router_probs * expert_along * (one_expert - my_prob)
        shared_logit_grad = shared_along * shared_weight * (1.0 - shared_weight)
        tail = jnp.concatenate([logit_grad, shared_logit_grad], axis=1)
        gate_grad = grad_hidden * up * sigmoid_gate * (1.0 + gate * (1.0 - sigmoid_gate))
        gate_grad = (
            gate_grad + jnp.pad(tail, ((0, 0), (hidden_width, spare - experts - 1)))
        ).astype(BF16)
        up_grad = (grad_hidden * gate * sigmoid_gate).astype(BF16)
        grad_down = grad_down + mm_tn(hidden_low, branch)
        grad_gate = grad_gate + mm_tn(everyone, gate_grad)
        grad_up = grad_up + mm_tn(everyone, up_grad)
        back_rows = mm_nt(gate_grad, gate_weight) + mm_nt(up_grad, up_weight)
        grad_parts.append(scatter_bits(back_rows.astype(BF16).reshape(lead + (width,)), bits))
        out_parts.append(
            scatter_bits(mm(hidden_low, down_weight).astype(BF16).reshape(lead + (width,)), bits)
        )
    live_rows = jnp.broadcast_to(live_own, (sequences, piece, 1)).reshape(rows, 1)
    moe_out = jnp.concatenate(out_parts).astype(F32)
    mixed = (residual + live_rows * moe_out).astype(BF16).reshape(tokens.shape)
    grad_normed = jnp.concatenate(grad_parts).astype(F32)
    grad_residual_in, grad_gain_moe = norm_back(grad_normed, normal_two, factor_two, gain_moe)
    grad_residual = grad_out.reshape(rows, width) + grad_residual_in

    attn_grad = (live_rows * grad_residual).astype(BF16).reshape(tokens.shape)
    attn_grad_parts = [
        gather_bits(value, bits)
        for value, bits in zip(
            pieces(deal(attn_grad, part, high).reshape(rows, width)), low_orders, strict=True
        )
    ]
    attended_grads = []
    grad_o = 0.0
    for value, ahead, bits in zip(attn_grad_parts, attended_parts, low_orders, strict=True):
        flat = value.reshape(-1, width)
        back = mm_nt(flat, o_rows).astype(BF16).reshape(value.shape[:-1] + (2 * HEAD,))
        attended_grads.append(to_order(back, bits, wanted))
        grad_o = grad_o + mm_tn(ahead, flat)
    attended_grad = jnp.concatenate(attended_grads, axis=-2)
    attended_grad = (
        attended_grad.reshape(8, parts, own_seq, piece, 2, HEAD)
        .transpose(2, 4, 0, 1, 3, 5)
        .reshape(own_seq, 2, length, HEAD)
    )
    again = jnp.exp(masked - log_total)
    prob_grad = jnp.einsum("shqd,shkd->shqk", attended_grad, values, preferred_element_type=F32)
    inner_sum = jnp.sum(again * prob_grad, axis=-1, keepdims=True)
    score_grad = (again * (prob_grad - inner_sum)).astype(BF16)
    grad_query = (
        jnp.einsum("shqk,shkd->shqd", score_grad, keys, preferred_element_type=F32) * score_scale
    )
    grad_key = (
        jnp.einsum("shqk,shqd->shkd", score_grad, queries, preferred_element_type=F32)
        * score_scale
    )
    grad_value = jnp.einsum("shqk,shqd->shkd", probs, attended_grad, preferred_element_type=F32)
    grads = jnp.stack(
        [
            rotate_back(grad_query, cosine, sine_table).astype(BF16),
            rotate_back(grad_key, cosine, sine_table).astype(BF16),
            grad_value.astype(BF16),
        ]
    )
    bias_grads = jnp.sum(grads.astype(F32), axis=(1, 3))
    grads_parts = to_parts(grads)
    grad_qkv = 0.0
    normed_grads = []
    for value, normed in zip(grads_parts, normed_parts, strict=True):
        normed_grads.append(mm_nt(value, qkv_weight))
        grad_qkv = grad_qkv + mm_tn(normed, value)
    grad_normed_one = reduce_low(normed_grads).astype(F32).reshape(rows, width)
    normal_one, factor_one = normalize(inputs.reshape(rows, width))
    grad_input, grad_gain_attn = norm_back(grad_normed_one, normal_one, factor_one, gain_attn)
    grad_tokens = (grad_residual + grad_input).astype(BF16).reshape(tokens.shape)

    grad_down = grad_down[:hidden_width].astype(BF16)

    def to_core(value, axis):
        low = lax.index_in_dim(value, 0, axis, keepdims=False)
        top = lax.index_in_dim(value, 1, axis, keepdims=False)
        keep = jnp.where(core == 0, low, top)
        give = jnp.where(core == 0, top, low)
        return keep.astype(F32) + swap(give, 0).astype(F32)

    grad_shared_down = to_core(grad_down[:shared_width].reshape(2, -1, width), 0)
    grad_expert_down = to_core(grad_down[shared_width:].reshape(2, -1, width), 0)
    tail_grads = grad_gate[:, hidden_width : hidden_width + experts + 1]
    grad_gu = jnp.stack(
        [grad_gate[:, :hidden_width].astype(BF16), grad_up[:, :hidden_width].astype(BF16)], axis=1
    )
    grad_shared_gu = to_core(
        grad_gu[:, :, :shared_width].reshape(chips, 2, depth, 2 * shared_width), 1
    ).astype(BF16)
    grad_shared_gu = lax.all_to_all(
        grad_shared_gu, CHIPS, split_axis=0, concat_axis=0, tiled=True
    )
    grad_shared_gu = (
        grad_shared_gu.reshape(chips, depth, 2, shared_width)
        .transpose(1, 2, 0, 3)
        .reshape(depth, -1)
        .astype(F32)
    )
    grad_expert_gu = to_core(
        grad_gu[:, :, shared_width:].reshape(2, 2, expert_rows, 2, expert_width), 1
    ).astype(BF16)
    keep_rows = jnp.where(x_bit == 0, grad_expert_gu[0], grad_expert_gu[1])
    give_rows = jnp.where(x_bit == 0, grad_expert_gu[1], grad_expert_gu[0])
    grad_expert_gu = by_bit(keep_rows, swap(give_rows, 1), x_bit, 2)
    grad_expert_gu = grad_expert_gu.reshape(1, expert_rows, -1).astype(F32)

    grad_qkv = to_core(grad_qkv.astype(BF16).reshape(width, 2, 3 * HEAD), 1).astype(BF16)
    grad_qkv = lax.all_to_all(
        grad_qkv.reshape(total, depth, 3 * HEAD), AXES, split_axis=0, concat_axis=0, tiled=True
    )
    grad_qkv = jnp.sum(grad_qkv.reshape(uppers, 16, depth, 3, HEAD).astype(F32), axis=0)
    grad_qkv = grad_qkv.transpose(2, 1, 0, 3).reshape(3, depth, width)
    grad_o = to_core(grad_o.astype(BF16).reshape(uppers, 2, depth, width), 1).astype(BF16)
    grad_o = xor_order(grad_o, upper)
    grad_o = sum(
        permute(grad_o[k], [(b, a) for a, b in places]).astype(F32)
        for k, places in enumerate(o_places)
    )

    bias_rows = lax.dynamic_update_slice_in_dim(
        jnp.zeros((3, heads // 2, 2 * HEAD), F32),
        bias_grads.reshape(3, 1, 2 * HEAD),
        pair,
        axis=1,
    ).reshape(3, width)
    vectors = jnp.concatenate(
        [grad_gain_attn[None], bias_rows, grad_gain_moe[None], tail_grads.T], axis=0
    )
    vectors = vectors.reshape(-1, total, depth).transpose(1, 0, 2)
    vectors = lax.psum_scatter(vectors, AXES, scatter_dimension=0, tiled=True)[0]
    return (
        mixed,
        grad_tokens,
        vectors[0],
        grad_qkv[0],
        grad_qkv[1],
        grad_qkv[2],
        vectors[1],
        vectors[2],
        vectors[3],
        grad_o,
        vectors[4],
        vectors[5 : 5 + experts].T,
        vectors[5 + experts],
        grad_shared_gu,
        grad_shared_down,
        grad_expert_gu,
        grad_expert_down[None],
    )


def solution(mesh):
    fine = Mesh(mesh.devices.reshape(mesh.devices.size // 4, 2, 2), AXES)
    given = P(None, AXES, None)
    rows = P(AXES, None)
    vector = P(AXES)
    expert = P("dp", ("x", "core"), None)
    in_specs = (
        given,
        given,
        P(),
        P(),
        P(),
        vector,
        rows,
        rows,
        rows,
        vector,
        vector,
        vector,
        rows,
        vector,
        rows,
        vector,
        rows,
        rows,
        expert,
        expert,
    )
    out_specs = (
        given,
        given,
        vector,
        rows,
        rows,
        rows,
        vector,
        vector,
        vector,
        rows,
        vector,
        rows,
        vector,
        rows,
        rows,
        expert,
        expert,
    )
    return jax.shard_map(
        on_device, mesh=fine, in_specs=in_specs, out_specs=out_specs, check_vma=False
    )
```

```python
import math

import jax
import jax.numpy as jnp
import numpy as np
from jax import lax
from jax.experimental import pallas as pl
from jax.experimental.pallas import tpu as pltpu
from jax.sharding import Mesh
from jax.sharding import PartitionSpec as P

HEAD = 128
TOP = 4
AXES = ("dp", "x", "core")
CHIPS = ("dp", "x")
SPLITS = (48, 40, 40)
LOW = (1, 2, 3)

epsilon = 1e-06
rope_base = 1000000.0
negative = -1e30
F32 = jnp.float32
BF16 = jnp.bfloat16


def mm(a, b):
    return lax.dot_general(a, b, (((1,), (0,)), ((), ())), preferred_element_type=F32)


def mm_tn(a, b):
    return lax.dot_general(a, b, (((0,), (0,)), ((), ())), preferred_element_type=F32)


def mm_nt(a, b):
    return lax.dot_general(a, b, (((1,), (1,)), ((), ())), preferred_element_type=F32)


def devices():
    return lax.axis_size("dp") * 4


def permute(value, pairs):
    return lax.ppermute(value, AXES, pairs)


def swap(value, bit):
    return permute(value, [(i, i ^ (1 << bit)) for i in range(devices())])


def gather_bits(value, bits):
    for bit in bits:
        value = jnp.stack([value, swap(value, bit)])
    return value


def add_low(a, b):
    return (a.astype(F32) + b.astype(F32)).astype(BF16)


def scatter_bits(value, bits):
    for bit in reversed(bits):
        value = add_low(value[0], swap(value[1], bit))
    return value


def pieces(rows):
    start = 0
    found = []
    for count in SPLITS:
        found.append(lax.slice_in_dim(rows, start, start + count, axis=-2))
        start += count
    return found


def rotations(high):
    return [high + (3, 1, 2), high + (1, 2, 3), high + (2, 3, 1)]


def to_order(value, bits, wanted):
    have = tuple(reversed(bits))
    lead = [have.index(bit) for bit in wanted]
    rest = list(range(len(bits), value.ndim))
    return value.transpose(lead + rest)


def relative(bits):
    found = np.zeros((1,), np.int64)
    for bit in bits:
        found = np.concatenate([found, found ^ (1 << bit)])
    return found


def by_bit(mine, theirs, flag, axis):
    low = jnp.where(flag == 0, mine, theirs)
    high = jnp.where(flag == 0, theirs, mine)
    return jnp.stack([low, high], axis=axis)


def xor_order(value, number):
    count = value.shape[0]
    return jnp.stack(
        [lax.dynamic_index_in_dim(value, number ^ k, 0, keepdims=False) for k in range(count)]
    )


def deal(value, part, high):
    parts = 2 << len(high)
    shape = value.shape
    value = xor_order(value.reshape((parts, shape[0] // parts) + shape[1:]), part)
    value = value.reshape((2,) * (len(high) + 1) + value.shape[1:])
    left = len(high) + 1
    for bit in tuple(reversed(high)) + (0,):
        left -= 1
        value = jnp.stack([value[0], swap(value[1], bit)], axis=left)
    return value


def undeal(value, part, high):
    done = 0
    for bit in (0,) + tuple(high):
        keep = lax.index_in_dim(value, 0, done, keepdims=False)
        give = lax.index_in_dim(value, 1, done, keepdims=False)
        value = jnp.stack([keep, swap(give, bit)])
        done += 1
    shape = value.shape[done:]
    value = xor_order(value.reshape((1 << done,) + shape), part)
    return value.reshape((value.shape[0] * shape[0],) + shape[1:])


def whole_kernel(body, outs, *operands):
    specs = [
        pl.BlockSpec(memory_space=pltpu.SMEM if value.dtype == jnp.int32 else pltpu.VMEM)
        for value in operands
    ]
    moved = sum(math.prod(value.shape) * value.dtype.itemsize for value in operands)
    moved += sum(math.prod(value.shape) * value.dtype.itemsize for value in outs)
    return pl.pallas_call(
        body,
        out_shape=outs,
        in_specs=specs,
        out_specs=[pl.BlockSpec(memory_space=pltpu.VMEM) for _ in outs],
        cost_estimate=pl.CostEstimate(flops=0, bytes_accessed=moved, transcendentals=0),
        compiler_params=pltpu.CompilerParams(vmem_limit_bytes=40 * 1024 * 1024),
    )(*operands)


def shape_of(dims, dtype=BF16):
    return jax.ShapeDtypeStruct(tuple(dims), dtype)


def split_heads(q_ref, k_ref, v_ref, out_ref):
    for place in range(out_ref.shape[0]):
        columns = pl.ds(place % 16 * HEAD, HEAD)
        for number, ref in enumerate((q_ref, k_ref, v_ref)):
            out_ref[place, :, number * HEAD : (number + 1) * HEAD] = ref[:, columns]


def join_heads(in_ref, q_ref, k_ref, v_ref):
    for head in range(16):
        for number, ref in enumerate((q_ref, k_ref, v_ref)):
            columns = slice(number * HEAD, (number + 1) * HEAD)
            total = in_ref[head, :, columns].astype(F32)
            for upper in range(1, in_ref.shape[0] // 16):
                total = total + in_ref[upper * 16 + head, :, columns].astype(F32)
            ref[:, head * HEAD : (head + 1) * HEAD] = total


def split_columns(in_ref, out_ref):
    count, rows, wide = out_ref.shape
    width = in_ref.shape[1] // (2 * count)
    tail = jnp.zeros((rows, wide // 2 - width), in_ref.dtype)
    for place in range(count):
        for side in range(2):
            start = (side * count + place) * width
            out_ref[place, :, side * wide // 2 : (side + 1) * wide // 2] = jnp.concatenate(
                [in_ref[:, start : start + width], tail], axis=1
            )


def join_columns(in_ref, out_ref):
    count, rows, wide = in_ref.shape
    width = out_ref.shape[1] // (2 * count)
    out_ref[...] = jnp.concatenate(
        [
            in_ref[place, :, side * wide // 2 : side * wide // 2 + width].astype(F32)
            for side in range(2)
            for place in range(count)
        ],
        axis=1,
    )


def join_halves(bit_ref, mine_ref, theirs_ref, out_ref):
    wide = mine_ref.shape[1]
    width = out_ref.shape[1] // 4
    mine = mine_ref[...].astype(F32)
    theirs = theirs_ref[...].astype(F32)
    first = jnp.where(bit_ref[0] == 0, mine, theirs)
    second = jnp.where(bit_ref[0] == 0, theirs, mine)
    out_ref[...] = jnp.concatenate(
        [
            half[:, side * wide // 2 : side * wide // 2 + width]
            for side in range(2)
            for half in (first, second)
        ],
        axis=1,
    )


def join_down(core_ref, shared_ref, shared_other, expert_ref, expert_other, out_ref):
    start = 0
    for ref, other, room in (
        (shared_ref, shared_other, -(-2 * shared_ref.shape[0] // 128) * 128),
        (expert_ref, expert_other, -(-2 * expert_ref.shape[0] // 128) * 128),
    ):
        count = ref.shape[0]
        mine = ref[...]
        theirs = other[...]
        out_ref[start : start + count, :] = jnp.where(core_ref[0] == 0, mine, theirs)
        out_ref[start + count : start + 2 * count, :] = jnp.where(core_ref[0] == 0, theirs, mine)
        out_ref[start + 2 * count : start + room, :] = jnp.zeros(
            (room - 2 * count, out_ref.shape[1]), out_ref.dtype
        )
        start += room


def join_gate_up(flags_ref, shared_ref, shared_other, expert_ref, expert_other, extra_ref, out_ref):
    chips, rows, shared_wide = shared_ref.shape
    core = flags_ref[0]
    for chip in range(chips):
        mine = shared_ref[chip]
        theirs = shared_other[chip]
        start = 2 * rows * chip
        out_ref[start : start + rows, :shared_wide] = jnp.where(core == 0, mine, theirs)
        out_ref[start + rows : start + 2 * rows, :shared_wide] = jnp.where(core == 0, theirs, mine)
    blocks = 512 // out_ref.shape[0]
    row_core = (pl.program_id(0) // blocks) & 1
    expert = jnp.where(row_core == core, expert_ref[0], expert_other[0])
    half = expert.shape[1] // 2
    out_ref[:, shared_wide:] = expert
    last = expert[:, half - 128 : half]
    out_ref[:, shared_wide + half - 128 : shared_wide + half] = last + extra_ref[...]


def assemble(flags, shared, shared_other, expert, expert_other, extra):
    chips, depth, shared_wide = shared.shape
    expert_wide = expert.shape[2]
    width = 2 * chips * depth
    block = 256
    per = block // (2 * depth)
    blocks = expert.shape[1] // block

    def expert_block(b, flags):
        return ((b // (2 * blocks)) ^ flags[1], b % blocks, 0)

    shared_spec = pl.BlockSpec((per, depth, shared_wide), lambda b, flags: (b, 0, 0))
    expert_spec = pl.BlockSpec((1, block, expert_wide), expert_block)
    wide = shared_wide + expert_wide
    return pl.pallas_call(
        join_gate_up,
        grid_spec=pltpu.PrefetchScalarGridSpec(
            num_scalar_prefetch=1,
            grid=(width // block,),
            in_specs=[
                shared_spec,
                shared_spec,
                expert_spec,
                expert_spec,
                pl.BlockSpec((block, 128), lambda b, flags: (b, 0)),
            ],
            out_specs=pl.BlockSpec((block, wide), lambda b, flags: (b, 0)),
        ),
        out_shape=shape_of((width, wide)),
        cost_estimate=pl.CostEstimate(
            flops=0, bytes_accessed=6 * width * wide, transcendentals=0
        ),
        compiler_params=pltpu.CompilerParams(vmem_limit_bytes=40 * 1024 * 1024),
    )(flags, shared, shared_other, expert, expert_other, extra)


def rotary_tables(positions):
    freq_index = jnp.arange(HEAD // 2).astype(F32)
    inverse = jnp.exp(freq_index * (-2.0 * math.log(rope_base) / HEAD))
    angles = positions.astype(F32)[:, None] * inverse[None, :]
    cosine = jnp.concatenate([jnp.cos(angles), jnp.cos(angles)], axis=-1)
    sine_table = jnp.concatenate([jnp.sin(angles), jnp.sin(angles)], axis=-1)
    return (cosine, sine_table)


def rotate(values, cosine, sine_table):
    half_width = HEAD // 2
    turned = jnp.concatenate([-values[..., half_width:], values[..., :half_width]], axis=-1)
    return values * cosine + turned * sine_table


def rotate_back(grads_in, cosine, sine_table):
    half_width = HEAD // 2
    scaled = grads_in * sine_table
    turned = jnp.concatenate([scaled[..., half_width:], -scaled[..., :half_width]], axis=-1)
    return grads_in * cosine + turned


def normalize(values):
    factor = lax.rsqrt(jnp.mean(values * values, axis=-1, keepdims=True) + epsilon)
    return (values * factor, factor)


def norm_back(grad_normed, normal, factor, gain_vector):
    scaled = grad_normed * gain_vector
    grad_input = factor * (scaled - normal * jnp.mean(scaled * normal, axis=-1, keepdims=True))
    return (grad_input, jnp.sum(grad_normed * normal, axis=0))


def on_device(
    tokens,
    cotangent,
    lengths,
    order,
    routes,
    norm_attn,
    q_weight,
    k_weight,
    v_weight,
    q_bias,
    k_bias,
    v_bias,
    o_weight,
    norm_moe,
    router,
    shared_gate,
    shared_gate_up,
    shared_down,
    expert_gate_up,
    expert_down,
):
    total = devices()
    chips = total // 2
    bit_count = total.bit_length() - 1
    high = tuple(range(4, bit_count))
    me = lax.axis_index(AXES)
    core = me & 1
    x_bit = (me >> 1) & 1
    pair = (me >> 1) & 7
    upper = me >> 4
    uppers = total // 16
    parts = 2 * uppers
    part = upper * 2 + core
    my_expert = me >> 2
    sequences, piece, width = tokens.shape
    experts = router.shape[1]
    rows = sequences * piece
    length = total * piece
    own_seq = sequences // parts
    depth = q_weight.shape[0]
    heads = width // HEAD
    shared_width = shared_down.shape[0] * total // chips
    expert_width = expert_down.shape[1] * 2
    shared_wide = -(-shared_width // 128) * 128
    expert_wide = -(-(expert_width + experts + 1) // 128) * 128
    padded = shared_wide + expert_wide
    tail_at = 2 * shared_wide + expert_width
    groups = total // 4
    per_group = sequences // groups
    group_rows = per_group * groups * piece
    capacity = (5 * group_rows * TOP + 4 * experts - 1) // (4 * experts)
    score_scale = HEAD ** (-0.5)
    low_orders = rotations(())
    full_orders = rotations(tuple(reversed(high)))

    small = jnp.concatenate(
        [
            jnp.stack([norm_attn, q_bias, k_bias, v_bias, norm_moe, shared_gate]),
            router.T,
            jnp.zeros((2, depth), BF16),
        ]
    )
    small = jnp.broadcast_to(small[None], (total,) + small.shape)
    small = lax.all_to_all(small, AXES, split_axis=0, concat_axis=0, tiled=True)
    small = small.transpose(1, 0, 2).reshape(small.shape[1], width)
    gain_attn = small[0].astype(F32)
    gain_moe = small[4].astype(F32)
    biases = lax.dynamic_slice_in_dim(small[1:4].reshape(3, heads // 2, 2, HEAD), pair, 1, axis=1)
    biases = biases[:, 0].transpose(1, 0, 2).astype(F32)

    token_parts = [
        gather_bits(value, bits)
        for value, bits in zip(
            pieces(deal(tokens, part, high).reshape(rows, width)), low_orders, strict=True
        )
    ]

    by_head = whole_kernel(
        split_heads, [shape_of((total, depth, 3 * HEAD))], q_weight, k_weight, v_weight
    )[0]
    my_head = lax.all_to_all(
        by_head, AXES, split_axis=0, concat_axis=0, tiled=True
    ).reshape(width, 3 * HEAD)
    other_head = swap(my_head, 0)
    qkv_weight = jnp.concatenate(
        [
            jnp.where(core == 0, my_head, other_head),
            jnp.where(core == 0, other_head, my_head),
        ],
        axis=1,
    )

    o_places = []
    for k in range(uppers):
        o_places.append(
            [
                (
                    i,
                    (((i % parts >> 1) ^ k) << 4) | ((i // parts) << 1) | (i & 1),
                )
                for i in range(total)
            ]
        )
    o_rows = xor_order(jnp.stack([permute(o_weight, places) for places in o_places]), upper)
    o_rows = by_bit(o_rows, swap(o_rows, 0), core, 1).reshape(2 * HEAD, width)

    own_positions = me * piece + jnp.arange(piece, dtype=jnp.int32)
    live_own = (own_positions[None, :] < lengths[:, None]).astype(F32)[:, :, None]
    grad_out = cotangent.astype(F32)
    branch_own = (live_own * grad_out).astype(BF16).reshape(rows, width)
    branch_parts = [
        gather_bits(value, bits)
        for value, bits in zip(pieces(branch_own), full_orders, strict=True)
    ]

    shared_pieces = whole_kernel(
        split_columns, [shape_of((chips, depth, 2 * shared_wide))], shared_gate_up
    )[0]
    shared_in = lax.all_to_all(shared_pieces, CHIPS, split_axis=0, concat_axis=0, tiled=True)
    shared_other = swap(shared_in, 0)
    expert_rows = expert_gate_up.shape[1]
    expert_halves = whole_kernel(
        split_columns, [shape_of((2, expert_rows, 2 * expert_wide))], expert_gate_up[0]
    )[0]
    keep_half = lax.dynamic_index_in_dim(expert_halves, x_bit, 0, keepdims=False)
    give_half = lax.dynamic_index_in_dim(expert_halves, 1 - x_bit, 0, keepdims=False)
    expert_in = jnp.stack([keep_half, swap(give_half, 1)])
    expert_other = swap(expert_in, 0)
    extra = jnp.concatenate(
        [
            jnp.zeros((expert_width - expert_wide + 128, width), BF16),
            small[6 : 6 + experts],
            small[5:6],
            jnp.zeros((expert_wide - expert_width - experts - 1, width), BF16),
        ]
    ).T
    gate_up_weight = assemble(
        jnp.stack([core, x_bit]), shared_in, shared_other, expert_in, expert_other, extra
    )
    down_weight = whole_kernel(
        join_down,
        [shape_of((padded, width))],
        core.reshape(1),
        shared_down,
        swap(shared_down, 0),
        expert_down[0],
        swap(expert_down[0], 0),
    )[0]

    all_positions = jnp.arange(length, dtype=jnp.int32)
    named = jnp.any(routes == my_expert, axis=-1) & (all_positions[None, :] < lengths[:, None])
    dealt = (
        jnp.take(named, order, axis=0)
        .reshape(groups, per_group, length // (4 * piece), 4, piece)
        .transpose(0, 3, 1, 2, 4)
        .reshape(groups * 4, group_rows)
        .astype(BF16)
    )
    index = jnp.arange(group_rows, dtype=jnp.int32)
    before = mm(dealt, (index[:, None] < index[None, :]).astype(BF16))
    kept = (
        jnp.where(before < capacity, dealt.astype(F32), 0.0)
        .reshape(groups, 4, per_group, length // (4 * piece), piece)
        .transpose(0, 2, 3, 1, 4)
        .reshape(sequences, length)
    )
    seq_index = jnp.arange(sequences, dtype=jnp.int32)
    place_of = jnp.sum(
        jnp.where(order[None, :] == seq_index[:, None], seq_index[None, :], 0), axis=1
    )
    kept = (
        jnp.take(kept, place_of, axis=0)
        .reshape(sequences, total, piece)
        .transpose(1, 0, 2)
        .reshape(total, rows)
    )

    wanted = (3, 2, 1)
    normed_parts = []
    projected = []
    for value, bits in zip(token_parts, low_orders, strict=True):
        flat = value.reshape(-1, width).astype(F32)
        normed = (normalize(flat)[0] * gain_attn).astype(BF16)
        normed_parts.append(normed)
        out = mm(normed, qkv_weight).reshape(value.shape[:-1] + (6 * HEAD,))
        projected.append(to_order(out, bits, wanted))
    shape_rows = (8, parts, own_seq, piece, 2, 3, HEAD)
    joined = jnp.concatenate(projected, axis=-2).reshape(shape_rows)
    joined = joined + biases
    joined = joined.transpose(5, 2, 4, 0, 1, 3, 6).reshape(3, own_seq, 2, length, HEAD)
    source = relative(tuple(reversed(high)) + (0,))
    low_relative = relative(LOW)
    rel = (low_relative[:, None] ^ source[None, :]).reshape(-1)
    positions = (
        (me ^ jnp.asarray(rel, jnp.int32))[:, None] * piece
        + jnp.arange(piece, dtype=jnp.int32)[None, :]
    ).reshape(-1)
    causal = positions[None, :] <= positions[:, None]
    cosine, sine_table = rotary_tables(positions)
    queries = rotate(joined[0], cosine, sine_table).astype(BF16)
    keys = rotate(joined[1], cosine, sine_table).astype(BF16)
    values = joined[2].astype(BF16)
    scores = (
        jnp.einsum("shqd,shkd->shqk", queries, keys, preferred_element_type=F32) * score_scale
    )
    masked = jnp.where(causal[None, None], scores, negative)
    top_score = jnp.max(masked, axis=-1, keepdims=True)
    log_total = top_score + jnp.log(jnp.sum(jnp.exp(masked - top_score), axis=-1, keepdims=True))
    probs = jnp.exp(masked - log_total).astype(BF16)
    attended = jnp.einsum("shqk,shkd->shqd", probs, values, preferred_element_type=F32)

    def to_parts(value):
        columns = value.shape[0]
        value = value.reshape(columns, own_seq, 2, 8, parts, piece, HEAD)
        value = value.transpose(3, 4, 1, 5, 2, 0, 6).reshape(2, 2, 2, rows, 2 * columns * HEAD)
        return [
            to_order(part_rows, (1, 2, 3), tuple(reversed(bits))).reshape(
                8 * part_rows.shape[-2], -1
            )
            for part_rows, bits in zip(pieces(value), low_orders, strict=True)
        ]

    def reduce_low(parts_in):
        found = [
            scatter_bits(value.astype(BF16).reshape(2, 2, 2, -1, width), bits)
            for value, bits in zip(parts_in, low_orders, strict=True)
        ]
        found = jnp.concatenate(found).reshape(
            (2,) * (1 + len(high)) + (own_seq, piece, width)
        )
        return undeal(found, part, high)

    attended_parts = to_parts(attended.astype(BF16)[None])
    attn_out = reduce_low([mm(value, o_rows) for value in attended_parts])
    inputs = tokens.astype(F32)
    residual = (inputs + live_own * attn_out.astype(F32)).reshape(rows, width)
    normal_two, factor_two = normalize(residual)
    normed_own = (normal_two * gain_moe).astype(BF16)

    expert_column = jnp.arange(experts, dtype=jnp.int32)[None, :]
    one_expert = (expert_column == my_expert).astype(F32)
    out_parts = []
    grad_parts = []
    grad_gate_up = grad_down = 0.0
    for normed, branch, bits, start in zip(
        pieces(normed_own), branch_parts, full_orders, (0, 48, 88), strict=True
    ):
        count = normed.shape[0]
        everyone = gather_bits(normed, bits)
        lead = everyone.shape[:-1]
        everyone = everyone.reshape(-1, width)
        branch = branch.reshape(-1, width)
        mask = jnp.take(
            kept[:, start : start + count], me ^ jnp.asarray(relative(bits), jnp.int32), axis=0
        ).reshape(-1, 1)
        joined_gu = mm(everyone, gate_up_weight)
        back = mm_nt(branch, down_weight)
        router_probs = jax.nn.softmax(joined_gu[:, tail_at : tail_at + experts], axis=-1)
        shared_weight = jax.nn.sigmoid(joined_gu[:, tail_at + experts : tail_at + experts + 1])
        my_prob = jnp.sum(router_probs * one_expert, axis=1, keepdims=True)
        hidden_low = []
        joined_grad = []
        alongs = []
        at = 0
        for wide, weight in ((shared_wide, shared_weight), (expert_wide, my_prob * mask)):
            gate = joined_gu[:, 2 * at : 2 * at + wide]
            up = joined_gu[:, 2 * at + wide : 2 * at + 2 * wide]
            back_part = back[:, at : at + wide]
            sigmoid_gate = jax.nn.sigmoid(gate)
            hidden = gate * sigmoid_gate * up
            hidden_low.append((hidden * weight).astype(BF16))
            alongs.append(jnp.sum(hidden * back_part, axis=1, keepdims=True))
            grad_hidden = back_part * weight
            joined_grad.append(
                grad_hidden * up * sigmoid_gate * (1.0 + gate * (1.0 - sigmoid_gate))
            )
            joined_grad.append(grad_hidden * gate * sigmoid_gate)
            at += wide
        logit_grad = router_probs * (alongs[1] * mask) * (one_expert - my_prob)
        shared_logit_grad = alongs[0] * shared_weight * (1.0 - shared_weight)
        tail = jnp.concatenate([logit_grad, shared_logit_grad], axis=1)
        joined_grad[2] = joined_grad[2] + jnp.pad(
            tail, ((0, 0), (expert_width, expert_wide - expert_width - experts - 1))
        )
        joined_grad = jnp.concatenate([value.astype(BF16) for value in joined_grad], axis=1)
        hidden_low = jnp.concatenate(hidden_low, axis=1)
        grad_down = grad_down + mm_tn(hidden_low, branch)
        grad_gate_up = grad_gate_up + mm_tn(everyone, joined_grad)
        back_rows = mm_nt(joined_grad, gate_up_weight)
        grad_parts.append(scatter_bits(back_rows.astype(BF16).reshape(lead + (width,)), bits))
        out_parts.append(
            scatter_bits(mm(hidden_low, down_weight).astype(BF16).reshape(lead + (width,)), bits)
        )
    live_rows = jnp.broadcast_to(live_own, (sequences, piece, 1)).reshape(rows, 1)
    moe_out = jnp.concatenate(out_parts).astype(F32)
    mixed = (residual + live_rows * moe_out).astype(BF16).reshape(tokens.shape)
    grad_normed = jnp.concatenate(grad_parts).astype(F32)
    grad_residual_in, grad_gain_moe = norm_back(grad_normed, normal_two, factor_two, gain_moe)
    grad_residual = grad_out.reshape(rows, width) + grad_residual_in

    attn_grad = (live_rows * grad_residual).astype(BF16).reshape(tokens.shape)
    attn_grad_parts = [
        gather_bits(value, bits)
        for value, bits in zip(
            pieces(deal(attn_grad, part, high).reshape(rows, width)), low_orders, strict=True
        )
    ]
    attended_grads = []
    grad_o = 0.0
    for value, ahead, bits in zip(attn_grad_parts, attended_parts, low_orders, strict=True):
        flat = value.reshape(-1, width)
        back = mm_nt(flat, o_rows).astype(BF16).reshape(value.shape[:-1] + (2 * HEAD,))
        attended_grads.append(to_order(back, bits, wanted))
        grad_o = grad_o + mm_tn(ahead, flat)
    attended_grad = jnp.concatenate(attended_grads, axis=-2)
    attended_grad = (
        attended_grad.reshape(8, parts, own_seq, piece, 2, HEAD)
        .transpose(2, 4, 0, 1, 3, 5)
        .reshape(own_seq, 2, length, HEAD)
    )
    again = jnp.exp(masked - log_total)
    prob_grad = jnp.einsum("shqd,shkd->shqk", attended_grad, values, preferred_element_type=F32)
    inner_sum = jnp.sum(again * prob_grad, axis=-1, keepdims=True)
    score_grad = (again * (prob_grad - inner_sum)).astype(BF16)
    grad_query = (
        jnp.einsum("shqk,shkd->shqd", score_grad, keys, preferred_element_type=F32) * score_scale
    )
    grad_key = (
        jnp.einsum("shqk,shqd->shkd", score_grad, queries, preferred_element_type=F32)
        * score_scale
    )
    grad_value = jnp.einsum("shqk,shqd->shkd", probs, attended_grad, preferred_element_type=F32)
    grads = jnp.stack(
        [
            rotate_back(grad_query, cosine, sine_table).astype(BF16),
            rotate_back(grad_key, cosine, sine_table).astype(BF16),
            grad_value.astype(BF16),
        ]
    )
    bias_grads = jnp.sum(grads.astype(F32), axis=(1, 3))
    grads_parts = to_parts(grads)
    grad_qkv = 0.0
    normed_grads = []
    for value, normed in zip(grads_parts, normed_parts, strict=True):
        normed_grads.append(mm_nt(value, qkv_weight))
        grad_qkv = grad_qkv + mm_tn(normed, value)
    grad_normed_one = reduce_low(normed_grads).astype(F32).reshape(rows, width)
    normal_one, factor_one = normalize(inputs.reshape(rows, width))
    grad_input, grad_gain_attn = norm_back(grad_normed_one, normal_one, factor_one, gain_attn)
    grad_tokens = (grad_residual + grad_input).astype(BF16).reshape(tokens.shape)

    def pick(value, axis, number):
        return lax.dynamic_index_in_dim(value, number, axis, keepdims=False)

    def to_core(value, axis):
        given_rows = swap(pick(value, axis, 1 - core), 0)
        return pick(value, axis, core).astype(F32) + given_rows.astype(F32)

    grad_down = grad_down.astype(BF16)
    grad_shared_down = to_core(grad_down[:shared_width].reshape(2, -1, width), 0)
    grad_expert_down = to_core(
        grad_down[shared_wide : shared_wide + expert_width].reshape(2, -1, width), 0
    )
    tail_grads = grad_gate_up[:, tail_at : tail_at + experts + 1]
    grad_gate_up = grad_gate_up.astype(BF16)
    grad_shared_gu = to_core(
        grad_gate_up[:, : 2 * shared_wide].reshape(chips, 2, depth, 2 * shared_wide), 1
    ).astype(BF16)
    grad_shared_gu = lax.all_to_all(
        grad_shared_gu, CHIPS, split_axis=0, concat_axis=0, tiled=True
    )
    grad_shared_gu = whole_kernel(
        join_columns, [shape_of((depth, 2 * chips * shared_width), F32)], grad_shared_gu
    )[0]
    grad_expert_gu = to_core(
        grad_gate_up[:, 2 * shared_wide :].reshape(2, 2, expert_rows, 2 * expert_wide), 1
    ).astype(BF16)
    grad_expert_gu = whole_kernel(
        join_halves,
        [shape_of((expert_rows, 4 * expert_width), F32)],
        x_bit.reshape(1),
        pick(grad_expert_gu, 0, x_bit),
        swap(pick(grad_expert_gu, 0, 1 - x_bit), 1),
    )[0][None]

    grad_qkv = grad_qkv.astype(BF16)
    low_head = grad_qkv[:, : 3 * HEAD]
    high_head = grad_qkv[:, 3 * HEAD :]
    given_head = swap(jnp.where(core == 0, high_head, low_head), 0)
    grad_qkv = add_low(jnp.where(core == 0, low_head, high_head), given_head)
    grad_qkv = lax.all_to_all(
        grad_qkv.reshape(total, depth, 3 * HEAD), AXES, split_axis=0, concat_axis=0, tiled=True
    )
    grad_qkv = whole_kernel(join_heads, [shape_of((depth, width), F32)] * 3, grad_qkv)
    grad_o = to_core(grad_o.astype(BF16).reshape(uppers, 2, depth, width), 1).astype(BF16)
    grad_o = xor_order(grad_o, upper)
    grad_o = sum(
        permute(grad_o[k], [(b, a) for a, b in places]).astype(F32)
        for k, places in enumerate(o_places)
    )

    bias_rows = lax.dynamic_update_slice_in_dim(
        jnp.zeros((3, heads // 2, 2 * HEAD), F32),
        bias_grads.reshape(3, 1, 2 * HEAD),
        pair,
        axis=1,
    ).reshape(3, width)

    def to_owners(vectors):
        vectors = vectors.reshape(-1, total, depth).transpose(1, 0, 2)
        vectors = lax.all_to_all(vectors, AXES, split_axis=0, concat_axis=0, tiled=True)
        return jnp.sum(vectors, axis=0)

    vectors = to_owners(jnp.concatenate([bias_rows, grad_gain_moe[None], tail_grads.T], axis=0))
    grad_gain_attn = to_owners(grad_gain_attn[None])[0]
    return (
        mixed,
        grad_tokens,
        grad_gain_attn,
        grad_qkv[0],
        grad_qkv[1],
        grad_qkv[2],
        vectors[0],
        vectors[1],
        vectors[2],
        grad_o,
        vectors[3],
        vectors[4 : 4 + experts].T,
        vectors[4 + experts],
        grad_shared_gu,
        grad_shared_down,
        grad_expert_gu,
        grad_expert_down[None],
    )


def solution(mesh):
    fine = Mesh(mesh.devices.reshape(mesh.devices.size // 4, 2, 2), AXES)
    given = P(None, AXES, None)
    rows = P(AXES, None)
    vector = P(AXES)
    expert = P("dp", ("x", "core"), None)
    in_specs = (
        given,
        given,
        P(),
        P(),
        P(),
        vector,
        rows,
        rows,
        rows,
        vector,
        vector,
        vector,
        rows,
        vector,
        rows,
        vector,
        rows,
        rows,
        expert,
        expert,
    )
    out_specs = (
        given,
        given,
        vector,
        rows,
        rows,
        rows,
        vector,
        vector,
        vector,
        rows,
        vector,
        rows,
        vector,
        rows,
        rows,
        expert,
        expert,
    )
    return jax.shard_map(
        on_device, mesh=fine, in_specs=in_specs, out_specs=out_specs, check_vma=False
    )
```

```python
import math

import jax
import jax.numpy as jnp
import numpy as np
from jax import lax
from jax.experimental import pallas as pl
from jax.experimental.pallas import tpu as pltpu
from jax.sharding import Mesh
from jax.sharding import PartitionSpec as P

HEAD = 128
TOP = 4
AXES = ("dp", "x", "core")
CHIPS = ("dp", "x")
SPLITS = (48, 40, 40)
PARTS = 1
LOW = (1, 2, 3)

epsilon = 1e-06
rope_base = 1000000.0
negative = -1e30
F32 = jnp.float32
BF16 = jnp.bfloat16


def mm(a, b):
    return lax.dot_general(a, b, (((1,), (0,)), ((), ())), preferred_element_type=F32)


def mm_tn(a, b):
    return lax.dot_general(a, b, (((0,), (0,)), ((), ())), preferred_element_type=F32)


def mm_nt(a, b):
    return lax.dot_general(a, b, (((1,), (1,)), ((), ())), preferred_element_type=F32)


def devices():
    return lax.axis_size("dp") * 4


def permute(value, pairs):
    return lax.ppermute(value, AXES, pairs)


def swap(value, bit):
    return permute(value, [(i, i ^ (1 << bit)) for i in range(devices())])


def gather_bits(value, bits):
    for bit in bits:
        value = jnp.stack([value, swap(value, bit)])
    return value


def add_low(a, b):
    return (a.astype(F32) + b.astype(F32)).astype(BF16)


def scatter_bits(value, bits):
    for bit in reversed(bits):
        value = add_low(value[0], swap(value[1], bit))
    return value


def after(value, *others):
    return lax.optimization_barrier((value, others))[0]


def pieces(rows):
    start = 0
    found = []
    for count in SPLITS:
        found.append(lax.slice_in_dim(rows, start, start + count, axis=-2))
        start += count
    return found


def rotations(high):
    return [high + (3, 1, 2), high + (1, 2, 3), high + (2, 3, 1)]


def to_order(value, bits, wanted):
    have = tuple(reversed(bits))
    lead = [have.index(bit) for bit in wanted]
    rest = list(range(len(bits), value.ndim))
    return value.transpose(lead + rest)


def relative(bits):
    found = np.zeros((1,), np.int64)
    for bit in bits:
        found = np.concatenate([found, found ^ (1 << bit)])
    return found


def by_bit(mine, theirs, flag, axis):
    low = jnp.where(flag == 0, mine, theirs)
    high = jnp.where(flag == 0, theirs, mine)
    return jnp.stack([low, high], axis=axis)


def xor_order(value, number):
    count = value.shape[0]
    return jnp.stack(
        [lax.dynamic_index_in_dim(value, number ^ k, 0, keepdims=False) for k in range(count)]
    )


def deal(value, part, high):
    parts = 2 << len(high)
    shape = value.shape
    value = xor_order(value.reshape((parts, shape[0] // parts) + shape[1:]), part)
    value = value.reshape((2,) * (len(high) + 1) + value.shape[1:])
    left = len(high) + 1
    for bit in tuple(reversed(high)) + (0,):
        left -= 1
        value = jnp.stack([value[0], swap(value[1], bit)], axis=left)
    return value


def undeal(value, part, high):
    done = 0
    for bit in (0,) + tuple(high):
        keep = lax.index_in_dim(value, 0, done, keepdims=False)
        give = lax.index_in_dim(value, 1, done, keepdims=False)
        value = jnp.stack([keep, swap(give, bit)])
        done += 1
    shape = value.shape[done:]
    value = xor_order(value.reshape((1 << done,) + shape), part)
    return value.reshape((value.shape[0] * shape[0],) + shape[1:])


def whole_kernel(body, outs, *operands):
    specs = [
        pl.BlockSpec(memory_space=pltpu.SMEM if value.dtype == jnp.int32 else pltpu.VMEM)
        for value in operands
    ]
    moved = sum(math.prod(value.shape) * value.dtype.itemsize for value in operands)
    moved += sum(math.prod(value.shape) * value.dtype.itemsize for value in outs)
    return pl.pallas_call(
        body,
        out_shape=outs,
        in_specs=specs,
        out_specs=[pl.BlockSpec(memory_space=pltpu.VMEM) for _ in outs],
        cost_estimate=pl.CostEstimate(flops=0, bytes_accessed=moved, transcendentals=0),
        compiler_params=pltpu.CompilerParams(vmem_limit_bytes=40 * 1024 * 1024),
    )(*operands)


def shape_of(dims, dtype=BF16):
    return jax.ShapeDtypeStruct(tuple(dims), dtype)


def split_heads(q_ref, k_ref, v_ref, out_ref):
    for place in range(out_ref.shape[0]):
        columns = pl.ds(place % 16 * HEAD, HEAD)
        for number, ref in enumerate((q_ref, k_ref, v_ref)):
            out_ref[place, :, number * HEAD : (number + 1) * HEAD] = ref[:, columns]


def join_heads(in_ref, q_ref, k_ref, v_ref):
    for head in range(16):
        for number, ref in enumerate((q_ref, k_ref, v_ref)):
            columns = slice(number * HEAD, (number + 1) * HEAD)
            total = in_ref[head, :, columns].astype(F32)
            for upper in range(1, in_ref.shape[0] // 16):
                total = total + in_ref[upper * 16 + head, :, columns].astype(F32)
            ref[:, head * HEAD : (head + 1) * HEAD] = total


def split_columns(in_ref, out_ref):
    count, rows, wide = out_ref.shape
    width = in_ref.shape[1] // (2 * count)
    tail = jnp.zeros((rows, wide // 2 - width), in_ref.dtype)
    for place in range(count):
        for side in range(2):
            start = (side * count + place) * width
            out_ref[place, :, side * wide // 2 : (side + 1) * wide // 2] = jnp.concatenate(
                [in_ref[:, start : start + width], tail], axis=1
            )


def join_columns(in_ref, out_ref):
    count, rows, wide = in_ref.shape
    width = out_ref.shape[1] // (2 * count)
    out_ref[...] = jnp.concatenate(
        [
            in_ref[place, :, side * wide // 2 : side * wide // 2 + width].astype(F32)
            for side in range(2)
            for place in range(count)
        ],
        axis=1,
    )


def join_halves(bit_ref, mine_ref, theirs_ref, out_ref):
    wide = mine_ref.shape[1]
    width = out_ref.shape[1] // 4
    mine = mine_ref[...].astype(F32)
    theirs = theirs_ref[...].astype(F32)
    first = jnp.where(bit_ref[0] == 0, mine, theirs)
    second = jnp.where(bit_ref[0] == 0, theirs, mine)
    out_ref[...] = jnp.concatenate(
        [
            half[:, side * wide // 2 : side * wide // 2 + width]
            for side in range(2)
            for half in (first, second)
        ],
        axis=1,
    )


def join_down(core_ref, shared_ref, shared_other, expert_ref, expert_other, out_ref):
    start = 0
    for ref, other, room in (
        (shared_ref, shared_other, -(-2 * shared_ref.shape[0] // 128) * 128),
        (expert_ref, expert_other, -(-2 * expert_ref.shape[0] // 128) * 128),
    ):
        count = ref.shape[0]
        mine = ref[...]
        theirs = other[...]
        out_ref[start : start + count, :] = jnp.where(core_ref[0] == 0, mine, theirs)
        out_ref[start + count : start + 2 * count, :] = jnp.where(core_ref[0] == 0, theirs, mine)
        out_ref[start + 2 * count : start + room, :] = jnp.zeros(
            (room - 2 * count, out_ref.shape[1]), out_ref.dtype
        )
        start += room


def join_gate_up(flags_ref, shared_ref, shared_other, expert_ref, expert_other, extra_ref, out_ref):
    chips, rows, shared_wide = shared_ref.shape
    core = flags_ref[0]
    for chip in range(chips):
        mine = shared_ref[chip]
        theirs = shared_other[chip]
        start = 2 * rows * chip
        out_ref[start : start + rows, :shared_wide] = jnp.where(core == 0, mine, theirs)
        out_ref[start + rows : start + 2 * rows, :shared_wide] = jnp.where(core == 0, theirs, mine)
    blocks = 512 // out_ref.shape[0]
    row_core = (pl.program_id(0) // blocks) & 1
    expert = jnp.where(row_core == core, expert_ref[0], expert_other[0])
    half = expert.shape[1] // 2
    out_ref[:, shared_wide:] = expert
    last = expert[:, half - 128 : half]
    out_ref[:, shared_wide + half - 128 : shared_wide + half] = last + extra_ref[...]


def assemble(flags, shared, shared_other, expert, expert_other, extra):
    chips, depth, shared_wide = shared.shape
    expert_wide = expert.shape[2]
    width = 2 * chips * depth
    block = 256
    per = block // (2 * depth)
    blocks = expert.shape[1] // block

    def expert_block(b, flags):
        return ((b // (2 * blocks)) ^ flags[1], b % blocks, 0)

    shared_spec = pl.BlockSpec((per, depth, shared_wide), lambda b, flags: (b, 0, 0))
    expert_spec = pl.BlockSpec((1, block, expert_wide), expert_block)
    wide = shared_wide + expert_wide
    return pl.pallas_call(
        join_gate_up,
        grid_spec=pltpu.PrefetchScalarGridSpec(
            num_scalar_prefetch=1,
            grid=(width // block,),
            in_specs=[
                shared_spec,
                shared_spec,
                expert_spec,
                expert_spec,
                pl.BlockSpec((block, 128), lambda b, flags: (b, 0)),
            ],
            out_specs=pl.BlockSpec((block, wide), lambda b, flags: (b, 0)),
        ),
        out_shape=shape_of((width, wide)),
        cost_estimate=pl.CostEstimate(
            flops=0, bytes_accessed=6 * width * wide, transcendentals=0
        ),
        compiler_params=pltpu.CompilerParams(vmem_limit_bytes=40 * 1024 * 1024),
    )(flags, shared, shared_other, expert, expert_other, extra)


def expert_kernel(
    sizes,
    expert_ref,
    rows_ref,
    branch_ref,
    mask_ref,
    gate_up_ref,
    down_ref,
    hidden_ref,
    grad_ref,
    out_ref,
    back_out,
    joined,
    back,
):
    shared_wide, expert_wide, tail_lane, experts = sizes
    padded = shared_wide + expert_wide
    joined[...] = mm(rows_ref[...], gate_up_ref[...])
    branch = branch_ref[...].reshape(rows_ref.shape)
    back[...] = mm_nt(branch, down_ref[...])

    tail_at = 2 * shared_wide + expert_wide - 128
    logits = joined[:, tail_at : tail_at + 128]
    lane = lax.broadcasted_iota(jnp.int32, logits.shape, 1)
    routed = (lane >= tail_lane) & (lane < tail_lane + experts)
    top = jnp.max(jnp.where(routed, logits, negative), axis=1, keepdims=True)
    powers = jnp.where(routed, jnp.exp(jnp.where(routed, logits - top, 0.0)), 0.0)
    router_probs = powers / jnp.sum(powers, axis=1, keepdims=True)
    one_expert = lane == tail_lane + expert_ref[0]
    my_prob = jnp.sum(jnp.where(one_expert, router_probs, 0.0), axis=1, keepdims=True)
    is_gate = lane == tail_lane + experts
    gate_logit = jnp.sum(jnp.where(is_gate, logits, 0.0), axis=1, keepdims=True)
    shared_weight = jax.nn.sigmoid(gate_logit)
    mask = mask_ref[...]
    alongs = []
    at = 0
    for wide, weight in ((shared_wide, shared_weight), (expert_wide, my_prob * mask)):
        along = jnp.zeros_like(my_prob)
        for start in range(0, wide, 128):
            gate_at = 2 * at + start
            gate = joined[:, gate_at : gate_at + 128]
            up = joined[:, gate_at + wide : gate_at + wide + 128]
            back_part = back[:, at + start : at + start + 128]
            sigmoid_gate = jax.nn.sigmoid(gate)
            silu = gate * sigmoid_gate
            hidden = silu * up
            hidden_ref[:, at + start : at + start + 128] = (hidden * weight).astype(BF16)
            along = along + jnp.sum(hidden * back_part, axis=1, keepdims=True)
            grad_hidden = back_part * weight
            gate_grad = grad_hidden * up * sigmoid_gate * (1.0 + gate * (1.0 - sigmoid_gate))
            grad_ref[:, gate_at + wide : gate_at + wide + 128] = (grad_hidden * silu).astype(BF16)
            if gate_at != tail_at:
                grad_ref[:, gate_at : gate_at + 128] = gate_grad.astype(BF16)
            else:
                tail_grad = gate_grad
        alongs.append(along)
        at += wide
    logit_grad = router_probs * (alongs[1] * mask) * (jnp.where(one_expert, 1.0, 0.0) - my_prob)
    shared_logit_grad = alongs[0] * shared_weight * (1.0 - shared_weight)
    tail_grad = tail_grad + jnp.where(is_gate, shared_logit_grad, logit_grad)
    grad_ref[:, tail_at : tail_at + 128] = tail_grad.astype(BF16)

    out_ref[...] = mm(hidden_ref[...], down_ref[...]).astype(BF16)
    back_out[...] = mm_nt(grad_ref[...], gate_up_ref[...]).astype(BF16)


def expert_pass(sizes, my_expert, part, rows, branch, mask, gate_up, down):
    shared_wide, expert_wide, _, _ = sizes
    padded = shared_wide + expert_wide
    count, width = rows.shape
    own = count // branch.shape[0]
    tile = 256
    once = dict(pipeline_mode=pl.Buffered(1))

    def at(i):
        return (i, 0)

    def fixed(i):
        return (0, 0)

    return pl.pallas_call(
        lambda *refs: expert_kernel(sizes, *refs),
        grid=(count // tile,),
        in_specs=[
            pl.BlockSpec(memory_space=pltpu.SMEM),
            pl.BlockSpec((tile, width), at),
            pl.BlockSpec((tile // own, own, width), lambda i: (i, part, 0)),
            pl.BlockSpec((tile, 1), at),
            pl.BlockSpec((width, 2 * padded), fixed, **once),
            pl.BlockSpec((padded, width), fixed, **once),
        ],
        out_specs=[
            pl.BlockSpec((tile, padded), at),
            pl.BlockSpec((tile, 2 * padded), at),
            pl.BlockSpec((tile, width), at),
            pl.BlockSpec((tile, width), at),
        ],
        out_shape=[
            shape_of((count, padded)),
            shape_of((count, 2 * padded)),
            shape_of((count, width)),
            shape_of((count, width)),
        ],
        scratch_shapes=[pltpu.VMEM((tile, 2 * padded), F32), pltpu.VMEM((tile, padded), F32)],
        cost_estimate=pl.CostEstimate(
            flops=count * width * padded,
            bytes_accessed=8 * count * width,
            transcendentals=0,
        ),
        compiler_params=pltpu.CompilerParams(vmem_limit_bytes=58 * 1024 * 1024),
    )(my_expert.reshape(1), rows, branch, mask, gate_up, down)


def rotary_tables(positions):
    freq_index = jnp.arange(HEAD // 2).astype(F32)
    inverse = jnp.exp(freq_index * (-2.0 * math.log(rope_base) / HEAD))
    angles = positions.astype(F32)[:, None] * inverse[None, :]
    cosine = jnp.concatenate([jnp.cos(angles), jnp.cos(angles)], axis=-1)
    sine_table = jnp.concatenate([jnp.sin(angles), jnp.sin(angles)], axis=-1)
    return (cosine, sine_table)


def rotate(values, cosine, sine_table):
    half_width = HEAD // 2
    turned = jnp.concatenate([-values[..., half_width:], values[..., :half_width]], axis=-1)
    return values * cosine + turned * sine_table


def rotate_back(grads_in, cosine, sine_table):
    half_width = HEAD // 2
    scaled = grads_in * sine_table
    turned = jnp.concatenate([scaled[..., half_width:], -scaled[..., :half_width]], axis=-1)
    return grads_in * cosine + turned


def normalize(values):
    factor = lax.rsqrt(jnp.mean(values * values, axis=-1, keepdims=True) + epsilon)
    return (values * factor, factor)


def norm_back(grad_normed, normal, factor, gain_vector):
    scaled = grad_normed * gain_vector
    grad_input = factor * (scaled - normal * jnp.mean(scaled * normal, axis=-1, keepdims=True))
    return (grad_input, jnp.sum(grad_normed * normal, axis=0))


def on_device(
    tokens,
    cotangent,
    lengths,
    order,
    routes,
    norm_attn,
    q_weight,
    k_weight,
    v_weight,
    q_bias,
    k_bias,
    v_bias,
    o_weight,
    norm_moe,
    router,
    shared_gate,
    shared_gate_up,
    shared_down,
    expert_gate_up,
    expert_down,
):
    total = devices()
    chips = total // 2
    bit_count = total.bit_length() - 1
    high = tuple(range(4, bit_count))
    me = lax.axis_index(AXES)
    core = me & 1
    x_bit = (me >> 1) & 1
    pair = (me >> 1) & 7
    upper = me >> 4
    uppers = total // 16
    parts = 2 * uppers
    part = upper * 2 + core
    my_expert = me >> 2
    sequences, piece, width = tokens.shape
    experts = router.shape[1]
    rows = sequences * piece
    length = total * piece
    own_seq = sequences // parts
    depth = q_weight.shape[0]
    heads = width // HEAD
    shared_width = shared_down.shape[0] * total // chips
    expert_width = expert_down.shape[1] * 2
    shared_wide = -(-shared_width // 128) * 128
    expert_wide = -(-(expert_width + experts + 1) // 128) * 128
    padded = shared_wide + expert_wide
    tail_at = 2 * shared_wide + expert_width
    groups = total // 4
    per_group = sequences // groups
    group_rows = per_group * groups * piece
    capacity = (5 * group_rows * TOP + 4 * experts - 1) // (4 * experts)
    score_scale = HEAD ** (-0.5)
    low_orders = rotations(())

    small = jnp.concatenate(
        [
            jnp.stack([norm_attn, q_bias, k_bias, v_bias, norm_moe, shared_gate]),
            router.T,
            jnp.zeros((2, depth), BF16),
        ]
    )
    small = jnp.broadcast_to(small[None], (total,) + small.shape)
    small = lax.all_to_all(small, AXES, split_axis=0, concat_axis=0, tiled=True)
    small = small.transpose(1, 0, 2).reshape(small.shape[1], width)
    gain_attn = small[0].astype(F32)
    gain_moe = small[4].astype(F32)
    biases = lax.dynamic_slice_in_dim(small[1:4].reshape(3, heads // 2, 2, HEAD), pair, 1, axis=1)
    biases = biases[:, 0].transpose(1, 0, 2).astype(F32)

    token_parts = [
        gather_bits(value, bits)
        for value, bits in zip(
            pieces(deal(tokens, part, high).reshape(rows, width)), low_orders, strict=True
        )
    ]

    by_head = whole_kernel(
        split_heads, [shape_of((total, depth, 3 * HEAD))], q_weight, k_weight, v_weight
    )[0]
    my_head = lax.all_to_all(
        by_head, AXES, split_axis=0, concat_axis=0, tiled=True
    ).reshape(width, 3 * HEAD)
    other_head = swap(my_head, 0)
    qkv_weight = jnp.concatenate(
        [
            jnp.where(core == 0, my_head, other_head),
            jnp.where(core == 0, other_head, my_head),
        ],
        axis=1,
    )

    o_places = []
    for k in range(uppers):
        o_places.append(
            [
                (
                    i,
                    (((i % parts >> 1) ^ k) << 4) | ((i // parts) << 1) | (i & 1),
                )
                for i in range(total)
            ]
        )
    o_rows = xor_order(jnp.stack([permute(o_weight, places) for places in o_places]), upper)
    o_rows = by_bit(o_rows, swap(o_rows, 0), core, 1).reshape(2 * HEAD, width)

    own_positions = me * piece + jnp.arange(piece, dtype=jnp.int32)
    live_own = (own_positions[None, :] < lengths[:, None]).astype(F32)[:, :, None]
    grad_out = cotangent.astype(F32)
    branch_own = (live_own * grad_out).astype(BF16).reshape(rows, width)
    branch_own = after(branch_own, *token_parts)
    branch_all = lax.all_gather(branch_own, CHIPS, axis=0)

    shared_pieces = whole_kernel(
        split_columns, [shape_of((chips, depth, 2 * shared_wide))], shared_gate_up
    )[0]
    shared_pieces = after(shared_pieces, *token_parts)
    shared_in = lax.all_to_all(shared_pieces, CHIPS, split_axis=0, concat_axis=0, tiled=True)
    shared_other = swap(shared_in, 0)
    expert_rows = expert_gate_up.shape[1]
    expert_halves = whole_kernel(
        split_columns, [shape_of((2, expert_rows, 2 * expert_wide))], expert_gate_up[0]
    )[0]
    keep_half = lax.dynamic_index_in_dim(expert_halves, x_bit, 0, keepdims=False)
    give_half = lax.dynamic_index_in_dim(expert_halves, 1 - x_bit, 0, keepdims=False)
    give_half = after(give_half, *token_parts)
    expert_in = jnp.stack([keep_half, swap(give_half, 1)])
    expert_other = swap(expert_in, 0)
    extra = jnp.concatenate(
        [
            jnp.zeros((expert_width - expert_wide + 128, width), BF16),
            small[6 : 6 + experts],
            small[5:6],
            jnp.zeros((expert_wide - expert_width - experts - 1, width), BF16),
        ]
    ).T
    gate_up_weight = assemble(
        jnp.stack([core, x_bit]), shared_in, shared_other, expert_in, expert_other, extra
    )
    down_weight = whole_kernel(
        join_down,
        [shape_of((padded, width))],
        core.reshape(1),
        shared_down,
        swap(shared_down, 0),
        expert_down[0],
        swap(expert_down[0], 0),
    )[0]

    all_positions = jnp.arange(length, dtype=jnp.int32)
    named = jnp.any(routes == my_expert, axis=-1) & (all_positions[None, :] < lengths[:, None])
    dealt = (
        jnp.take(named, order, axis=0)
        .reshape(groups, per_group, length // (4 * piece), 4, piece)
        .transpose(0, 3, 1, 2, 4)
        .reshape(groups * 4, group_rows)
        .astype(BF16)
    )
    index = jnp.arange(group_rows, dtype=jnp.int32)
    before = mm(dealt, (index[:, None] < index[None, :]).astype(BF16))
    kept = (
        jnp.where(before < capacity, dealt.astype(F32), 0.0)
        .reshape(groups, 4, per_group, length // (4 * piece), piece)
        .transpose(0, 2, 3, 1, 4)
        .reshape(sequences, length)
    )
    seq_index = jnp.arange(sequences, dtype=jnp.int32)
    place_of = jnp.sum(
        jnp.where(order[None, :] == seq_index[:, None], seq_index[None, :], 0), axis=1
    )
    kept = (
        jnp.take(kept, place_of, axis=0)
        .reshape(sequences, total, piece)
        .transpose(1, 0, 2)
        .reshape(total, rows)
    )

    wanted = (3, 2, 1)
    normed_parts = []
    projected = []
    for value, bits in zip(token_parts, low_orders, strict=True):
        flat = value.reshape(-1, width).astype(F32)
        normed = (normalize(flat)[0] * gain_attn).astype(BF16)
        normed_parts.append(normed)
        out = mm(normed, qkv_weight).reshape(value.shape[:-1] + (6 * HEAD,))
        projected.append(to_order(out, bits, wanted))
    shape_rows = (8, parts, own_seq, piece, 2, 3, HEAD)
    joined = jnp.concatenate(projected, axis=-2).reshape(shape_rows)
    joined = joined + biases
    joined = joined.transpose(5, 2, 4, 0, 1, 3, 6).reshape(3, own_seq, 2, length, HEAD)
    source = relative(tuple(reversed(high)) + (0,))
    low_relative = relative(LOW)
    rel = (low_relative[:, None] ^ source[None, :]).reshape(-1)
    positions = (
        (me ^ jnp.asarray(rel, jnp.int32))[:, None] * piece
        + jnp.arange(piece, dtype=jnp.int32)[None, :]
    ).reshape(-1)
    causal = positions[None, :] <= positions[:, None]
    cosine, sine_table = rotary_tables(positions)
    queries = rotate(joined[0], cosine, sine_table).astype(BF16)
    keys = rotate(joined[1], cosine, sine_table).astype(BF16)
    values = joined[2].astype(BF16)
    scores = (
        jnp.einsum("shqd,shkd->shqk", queries, keys, preferred_element_type=F32) * score_scale
    )
    masked = jnp.where(causal[None, None], scores, negative)
    top_score = jnp.max(masked, axis=-1, keepdims=True)
    log_total = top_score + jnp.log(jnp.sum(jnp.exp(masked - top_score), axis=-1, keepdims=True))
    probs = jnp.exp(masked - log_total).astype(BF16)
    attended = jnp.einsum("shqk,shkd->shqd", probs, values, preferred_element_type=F32)

    def to_parts(value):
        columns = value.shape[0]
        value = value.reshape(columns, own_seq, 2, 8, parts, piece, HEAD)
        value = value.transpose(3, 4, 1, 5, 2, 0, 6).reshape(2, 2, 2, rows, 2 * columns * HEAD)
        return [
            to_order(part_rows, (1, 2, 3), tuple(reversed(bits))).reshape(
                8 * part_rows.shape[-2], -1
            )
            for part_rows, bits in zip(pieces(value), low_orders, strict=True)
        ]

    def reduce_low(parts_in):
        found = [
            scatter_bits(value.astype(BF16).reshape(2, 2, 2, -1, width), bits)
            for value, bits in zip(parts_in, low_orders, strict=True)
        ]
        found = jnp.concatenate(found).reshape(
            (2,) * (1 + len(high)) + (own_seq, piece, width)
        )
        return found

    attended_parts = to_parts(attended.astype(BF16)[None])
    attn_out = undeal(
        reduce_low([mm(value, o_rows) for value in attended_parts]), part, high
    )
    attn_out = after(attn_out, branch_all)
    inputs = tokens.astype(F32)
    residual = (inputs + live_own * attn_out.astype(F32)).reshape(rows, width)
    normal_two, factor_two = normalize(residual)
    normed_own = (normal_two * gain_moe).astype(BF16)

    expert_column = jnp.arange(experts, dtype=jnp.int32)[None, :]
    one_expert = (expert_column == my_expert).astype(F32)
    own_rows = rows // PARTS
    everyone = [
        lax.all_gather(
            normed_own[number * own_rows : (number + 1) * own_rows], CHIPS, axis=0, tiled=True
        )
        for number in range(PARTS)
    ]
    kept = kept.reshape(chips, 2, PARTS, own_rows)
    kept = lax.dynamic_index_in_dim(kept, core, 1, keepdims=False)
    masks = [kept[:, number].reshape(-1, 1) for number in range(PARTS)]
    branch = [
        branch_all[:, number * own_rows : (number + 1) * own_rows].reshape(-1, width)
        for number in range(PARTS)
    ]

    sizes = (shared_wide, expert_wide, expert_width - expert_wide + 128, experts)

    def expert_part(number, *others):
        return expert_pass(
            sizes,
            my_expert,
            number,
            after(everyone[number], *others),
            branch_all,
            masks[number],
            gate_up_weight,
            down_weight,
        )

    def reduce(value):
        return lax.psum_scatter(value, CHIPS, scatter_dimension=0, tiled=True)

    def weight_grad(number, total_grad, *others):
        return total_grad + mm_tn(everyone[number], after(joined[number], total_grad, *others))

    def down_grad(number, total_grad, *others):
        return total_grad + mm_tn(after(hidden[number], total_grad, *others), branch[number])

    hidden = [None] * PARTS
    joined = [None] * PARTS
    outs = [None] * PARTS
    grad_parts = [None] * PARTS
    before_it = ()
    for number in range(PARTS):
        hidden[number], joined[number], outs[number], back_rows = expert_part(number, *before_it)
        grad_parts[number] = reduce(back_rows)
        before_it = (joined[number],)
    grad_gate_up = 0.0
    grad_down = 0.0
    for number in range(PARTS):
        grad_gate_up = weight_grad(number, grad_gate_up, joined[-1], *grad_parts[:-1])
    for number in range(PARTS):
        grad_down = down_grad(number, grad_down, grad_gate_up)
    live_rows = jnp.broadcast_to(live_own, (sequences, piece, 1)).reshape(rows, 1)
    grad_normed = jnp.concatenate(grad_parts).astype(F32)
    grad_residual_in, grad_gain_moe = norm_back(grad_normed, normal_two, factor_two, gain_moe)
    grad_residual = grad_out.reshape(rows, width) + grad_residual_in

    attn_grad = (live_rows * grad_residual).astype(BF16).reshape(tokens.shape)
    attn_grad_parts = [
        gather_bits(value, bits)
        for value, bits in zip(
            pieces(deal(attn_grad, part, high).reshape(rows, width)), low_orders, strict=True
        )
    ]
    attn_grad_parts[0] = after(attn_grad_parts[0], grad_down)
    attended_grads = []
    grad_o = 0.0
    for value, ahead, bits in zip(attn_grad_parts, attended_parts, low_orders, strict=True):
        flat = value.reshape(-1, width)
        back = mm_nt(flat, o_rows).astype(BF16).reshape(value.shape[:-1] + (2 * HEAD,))
        attended_grads.append(to_order(back, bits, wanted))
        grad_o = grad_o + mm_tn(ahead, flat)
    outs = [after(value, *attn_grad_parts) for value in outs]
    moe_out = jnp.concatenate([reduce(value) for value in outs]).astype(F32)

    def pick(value, axis, number):
        return lax.dynamic_index_in_dim(value, number, axis, keepdims=False)

    def to_core(value, axis):
        given_rows = swap(pick(value, axis, 1 - core), 0)
        return pick(value, axis, core).astype(F32) + given_rows.astype(F32)

    def to_owners(vectors):
        vectors = vectors.reshape(-1, total, depth).transpose(1, 0, 2)
        vectors = lax.all_to_all(vectors, AXES, split_axis=0, concat_axis=0, tiled=True)
        return jnp.sum(vectors, axis=0)

    tail_grads = grad_gate_up[:, tail_at : tail_at + experts + 1]
    grad_gate_up = grad_gate_up.astype(BF16)
    grad_shared_gu = to_core(
        grad_gate_up[:, : 2 * shared_wide].reshape(chips, 2, depth, 2 * shared_wide), 1
    ).astype(BF16)
    grad_expert_gu = to_core(
        grad_gate_up[:, 2 * shared_wide :].reshape(2, 2, expert_rows, 2 * expert_wide), 1
    ).astype(BF16)
    grad_down = grad_down.astype(BF16)
    grad_shared_down = to_core(grad_down[:shared_width].reshape(2, -1, width), 0)
    grad_expert_down = to_core(
        grad_down[shared_wide : shared_wide + expert_width].reshape(2, -1, width), 0
    )
    vectors = to_owners(jnp.concatenate([grad_gain_moe[None], tail_grads.T], axis=0))
    attended_grad = after(
        jnp.concatenate(attended_grads, axis=-2), grad_shared_gu, grad_expert_gu
    )
    grad_shared_gu = lax.all_to_all(
        grad_shared_gu, CHIPS, split_axis=0, concat_axis=0, tiled=True
    )
    mine_gu = pick(grad_expert_gu, 0, x_bit)
    theirs_gu = swap(pick(grad_expert_gu, 0, 1 - x_bit), 1)
    grad_o = to_core(grad_o.astype(BF16).reshape(uppers, 2, depth, width), 1).astype(BF16)
    grad_o = xor_order(grad_o, upper)
    grad_o = sum(
        permute(grad_o[k], [(b, a) for a, b in places]).astype(F32)
        for k, places in enumerate(o_places)
    )
    attended_grad = (
        attended_grad.reshape(8, parts, own_seq, piece, 2, HEAD)
        .transpose(2, 4, 0, 1, 3, 5)
        .reshape(own_seq, 2, length, HEAD)
    )
    again = jnp.exp(masked - log_total)
    prob_grad = jnp.einsum("shqd,shkd->shqk", attended_grad, values, preferred_element_type=F32)
    inner_sum = jnp.sum(again * prob_grad, axis=-1, keepdims=True)
    score_grad = (again * (prob_grad - inner_sum)).astype(BF16)
    grad_query = (
        jnp.einsum("shqk,shkd->shqd", score_grad, keys, preferred_element_type=F32) * score_scale
    )
    grad_key = (
        jnp.einsum("shqk,shqd->shkd", score_grad, queries, preferred_element_type=F32)
        * score_scale
    )
    grad_value = jnp.einsum("shqk,shqd->shkd", probs, attended_grad, preferred_element_type=F32)
    grads = jnp.stack(
        [
            rotate_back(grad_query, cosine, sine_table).astype(BF16),
            rotate_back(grad_key, cosine, sine_table).astype(BF16),
            grad_value.astype(BF16),
        ]
    )
    grads = after(grads, vectors)
    bias_grads = jnp.sum(grads.astype(F32), axis=(1, 3))
    grads_parts = to_parts(grads)
    grad_qkv = 0.0
    for value, normed in zip(grads_parts, normed_parts, strict=True):
        grad_qkv = grad_qkv + mm_tn(normed, value)
    grad_qkv = grad_qkv.astype(BF16)
    low_head = grad_qkv[:, : 3 * HEAD]
    high_head = grad_qkv[:, 3 * HEAD :]
    give_head = jnp.where(core == 0, high_head, low_head)
    grads_parts[0] = after(grads_parts[0], give_head)
    keep_head = jnp.where(core == 0, low_head, high_head)
    grad_qkv = lax.all_to_all(
        add_low(keep_head, swap(give_head, 0)).reshape(total, depth, 3 * HEAD),
        AXES,
        split_axis=0,
        concat_axis=0,
        tiled=True,
    )
    grad_normed_one = reduce_low([mm_nt(value, qkv_weight) for value in grads_parts])
    grad_normed_one = after(grad_normed_one, grad_shared_gu, theirs_gu, grad_o)
    grad_normed_one = undeal(grad_normed_one, part, high).astype(F32).reshape(rows, width)
    grad_qkv = whole_kernel(join_heads, [shape_of((depth, width), F32)] * 3, grad_qkv)
    grad_shared_gu = whole_kernel(
        join_columns, [shape_of((depth, 2 * chips * shared_width), F32)], grad_shared_gu
    )[0]
    grad_expert_gu = whole_kernel(
        join_halves,
        [shape_of((expert_rows, 4 * expert_width), F32)],
        x_bit.reshape(1),
        mine_gu,
        theirs_gu,
    )[0][None]
    normal_one, factor_one = normalize(inputs.reshape(rows, width))
    grad_input, grad_gain_attn = norm_back(grad_normed_one, normal_one, factor_one, gain_attn)
    grad_tokens = (grad_residual + grad_input).astype(BF16).reshape(tokens.shape)
    mixed = (residual + live_rows * moe_out).astype(BF16).reshape(tokens.shape)

    bias_rows = lax.dynamic_update_slice_in_dim(
        jnp.zeros((3, heads // 2, 2 * HEAD), F32),
        bias_grads.reshape(3, 1, 2 * HEAD),
        pair,
        axis=1,
    ).reshape(3, width)
    ends = to_owners(jnp.concatenate([bias_rows, grad_gain_attn[None]], axis=0))
    return (
        mixed,
        grad_tokens,
        ends[3],
        grad_qkv[0],
        grad_qkv[1],
        grad_qkv[2],
        ends[0],
        ends[1],
        ends[2],
        grad_o,
        vectors[0],
        vectors[1 : 1 + experts].T,
        vectors[1 + experts],
        grad_shared_gu,
        grad_shared_down,
        grad_expert_gu,
        grad_expert_down[None],
    )


def solution(mesh):
    fine = Mesh(mesh.devices.reshape(mesh.devices.size // 4, 2, 2), AXES)
    given = P(None, AXES, None)
    rows = P(AXES, None)
    vector = P(AXES)
    expert = P("dp", ("x", "core"), None)
    in_specs = (
        given,
        given,
        P(),
        P(),
        P(),
        vector,
        rows,
        rows,
        rows,
        vector,
        vector,
        vector,
        rows,
        vector,
        rows,
        vector,
        rows,
        rows,
        expert,
        expert,
    )
    out_specs = (
        given,
        given,
        vector,
        rows,
        rows,
        rows,
        vector,
        vector,
        vector,
        rows,
        vector,
        rows,
        vector,
        rows,
        rows,
        expert,
        expert,
    )
    return jax.shard_map(
        on_device, mesh=fine, in_specs=in_specs, out_specs=out_specs, check_vma=False
    )
```

```python
import math

import jax
import jax.numpy as jnp
import numpy as np
from jax import lax
from jax.experimental import pallas as pl
from jax.experimental.pallas import tpu as pltpu
from jax.sharding import Mesh
from jax.sharding import PartitionSpec as P

HEAD = 128
TOP = 4
AXES = ("dp", "x", "core")
CHIPS = ("dp", "x")
SPLITS = (48, 40, 40)
LOW = (1, 2, 3)

epsilon = 1e-06
rope_base = 1000000.0
negative = -1e30
F32 = jnp.float32
BF16 = jnp.bfloat16


def mm(a, b):
    return lax.dot_general(a, b, (((1,), (0,)), ((), ())), preferred_element_type=F32)


def mm_tn(a, b):
    return lax.dot_general(a, b, (((0,), (0,)), ((), ())), preferred_element_type=F32)


def mm_nt(a, b):
    return lax.dot_general(a, b, (((1,), (1,)), ((), ())), preferred_element_type=F32)


def devices():
    return lax.axis_size("dp") * 4


def permute(value, pairs):
    return lax.ppermute(value, AXES, pairs)


def swap(value, bit):
    return permute(value, [(i, i ^ (1 << bit)) for i in range(devices())])


def gather_bits(value, bits):
    for bit in bits:
        value = jnp.stack([value, swap(value, bit)])
    return value


def add_low(a, b):
    return (a.astype(F32) + b.astype(F32)).astype(BF16)


def scatter_bits(value, bits):
    for bit in reversed(bits):
        value = add_low(value[0], swap(value[1], bit))
    return value


def after(value, *others):
    return lax.optimization_barrier((value, others))[0]


def together(*lists):
    return lax.optimization_barrier(tuple(tuple(values) for values in lists))


def gather_parts(parts, orders):
    parts = list(parts)
    for step in range(len(orders[0])):
        got = [swap(part, order[step]) for part, order in zip(parts, orders, strict=True)]
        parts = [jnp.stack(pair) for pair in zip(*together(parts, got), strict=True)]
    return parts


def rest_of(high, order):
    return tuple(reversed(high)) + order


class Gather:
    def __init__(self, rows, high):
        self.value = gather_bits(rows, tuple(reversed(high)))

    def split(self):
        self.parts = pieces(self.value)
        self.orders = rotations(())

    def step(self):
        got = [swap(part, order[0]) for part, order in zip(self.parts, self.orders, strict=True)]
        self.pairs = list(zip(*together(self.parts, got), strict=True))
        self.orders = [order[1:] for order in self.orders]
        self.parts = [jnp.stack(pair) for pair in self.pairs]
        return got

    def whole(self):
        width = self.value.shape[-1]
        return jnp.concatenate([half.reshape(-1, width) for pair in self.pairs for half in pair])


class Reduction:
    def __init__(self, value, high, chips):
        self.high = tuple(reversed(high))
        self.bits = [order[::-1] for order in rotations(())]
        width = value.shape[-1]
        start = 0
        self.keep = []
        self.give = []
        for count in SPLITS:
            half = chips // 2 * count
            shape = (2,) * (2 + len(high)) + (count, width)
            self.keep.append(value[start : start + half].reshape(shape))
            self.give.append(value[start + half : start + 2 * half].reshape(shape))
            start += 2 * half

    def send(self, *others):
        give = after(tuple(self.give), *others) if others else self.give
        self.got = [swap(part, bits[0]) for part, bits in zip(give, self.bits, strict=True)]
        self.bits = [bits[1:] for bits in self.bits]
        return self.got

    def add(self):
        keeps, gots = together(self.keep, self.got)
        parts = [add_low(keep, got) for keep, got in zip(keeps, gots, strict=True)]
        if self.bits[0]:
            self.keep = [part[0] for part in parts]
            self.give = [part[1] for part in parts]
        else:
            self.value = jnp.concatenate(parts, axis=-2)

    def finish(self):
        return scatter_bits(self.value, self.high)


def pieces(rows):
    start = 0
    found = []
    for count in SPLITS:
        found.append(lax.slice_in_dim(rows, start, start + count, axis=-2))
        start += count
    return found


def rotations(high):
    return [high + (3, 1, 2), high + (1, 2, 3), high + (2, 3, 1)]


def to_order(value, bits, wanted):
    have = tuple(reversed(bits))
    lead = [have.index(bit) for bit in wanted]
    rest = list(range(len(bits), value.ndim))
    return value.transpose(lead + rest)


def relative(bits):
    found = np.zeros((1,), np.int64)
    for bit in bits:
        found = np.concatenate([found, found ^ (1 << bit)])
    return found


def by_bit(mine, theirs, flag, axis):
    low = jnp.where(flag == 0, mine, theirs)
    high = jnp.where(flag == 0, theirs, mine)
    return jnp.stack([low, high], axis=axis)


def xor_order(value, number):
    count = value.shape[0]
    return jnp.stack(
        [lax.dynamic_index_in_dim(value, number ^ k, 0, keepdims=False) for k in range(count)]
    )


def deal(value, part, high):
    parts = 2 << len(high)
    shape = value.shape
    value = xor_order(value.reshape((parts, shape[0] // parts) + shape[1:]), part)
    value = value.reshape((2,) * (len(high) + 1) + value.shape[1:])
    left = len(high) + 1
    arrived = []
    for bit in tuple(reversed(high)) + (0,):
        left -= 1
        arrived.append(swap(value[1], bit))
        value = jnp.stack([value[0], arrived[-1]], axis=left)
    return value, arrived


def undeal(value, part, high):
    done = 0
    for bit in (0,) + tuple(high):
        keep = lax.index_in_dim(value, 0, done, keepdims=False)
        give = lax.index_in_dim(value, 1, done, keepdims=False)
        value = jnp.stack([keep, swap(give, bit)])
        done += 1
    shape = value.shape[done:]
    value = xor_order(value.reshape((1 << done,) + shape), part)
    return value.reshape((value.shape[0] * shape[0],) + shape[1:])


def whole_kernel(body, outs, *operands):
    specs = [
        pl.BlockSpec(memory_space=pltpu.SMEM if value.dtype == jnp.int32 else pltpu.VMEM)
        for value in operands
    ]
    moved = sum(math.prod(value.shape) * value.dtype.itemsize for value in operands)
    moved += sum(math.prod(value.shape) * value.dtype.itemsize for value in outs)
    return pl.pallas_call(
        body,
        out_shape=outs,
        in_specs=specs,
        out_specs=[pl.BlockSpec(memory_space=pltpu.VMEM) for _ in outs],
        cost_estimate=pl.CostEstimate(flops=0, bytes_accessed=moved, transcendentals=0),
        compiler_params=pltpu.CompilerParams(vmem_limit_bytes=40 * 1024 * 1024),
    )(*operands)


def shape_of(dims, dtype=BF16):
    return jax.ShapeDtypeStruct(tuple(dims), dtype)


def split_heads(q_ref, k_ref, v_ref, out_ref):
    for place in range(out_ref.shape[0]):
        columns = pl.ds(place % 16 * HEAD, HEAD)
        for number, ref in enumerate((q_ref, k_ref, v_ref)):
            out_ref[place, :, number * HEAD : (number + 1) * HEAD] = ref[:, columns]


def join_heads(in_ref, q_ref, k_ref, v_ref):
    for head in range(16):
        for number, ref in enumerate((q_ref, k_ref, v_ref)):
            columns = slice(number * HEAD, (number + 1) * HEAD)
            total = in_ref[head, :, columns].astype(F32)
            for upper in range(1, in_ref.shape[0] // 16):
                total = total + in_ref[upper * 16 + head, :, columns].astype(F32)
            ref[:, head * HEAD : (head + 1) * HEAD] = total


def split_columns(in_ref, out_ref):
    count, rows, wide = out_ref.shape
    width = in_ref.shape[1] // (2 * count)
    tail = jnp.zeros((rows, wide // 2 - width), in_ref.dtype)
    for place in range(count):
        for side in range(2):
            start = (side * count + place) * width
            out_ref[place, :, side * wide // 2 : (side + 1) * wide // 2] = jnp.concatenate(
                [in_ref[:, start : start + width], tail], axis=1
            )


def join_columns(in_ref, out_ref):
    count, rows, wide = in_ref.shape
    width = out_ref.shape[1] // (2 * count)
    out_ref[...] = jnp.concatenate(
        [
            in_ref[place, :, side * wide // 2 : side * wide // 2 + width].astype(F32)
            for side in range(2)
            for place in range(count)
        ],
        axis=1,
    )


def join_halves(bit_ref, mine_ref, theirs_ref, out_ref):
    wide = mine_ref.shape[1]
    width = out_ref.shape[1] // 4
    mine = mine_ref[...].astype(F32)
    theirs = theirs_ref[...].astype(F32)
    first = jnp.where(bit_ref[0] == 0, mine, theirs)
    second = jnp.where(bit_ref[0] == 0, theirs, mine)
    out_ref[...] = jnp.concatenate(
        [
            half[:, side * wide // 2 : side * wide // 2 + width]
            for side in range(2)
            for half in (first, second)
        ],
        axis=1,
    )


def join_down(core_ref, shared_ref, shared_other, expert_ref, expert_other, out_ref):
    start = 0
    for ref, other, room in (
        (shared_ref, shared_other, -(-2 * shared_ref.shape[0] // 128) * 128),
        (expert_ref, expert_other, -(-2 * expert_ref.shape[0] // 128) * 128),
    ):
        count = ref.shape[0]
        mine = ref[...]
        theirs = other[...]
        out_ref[start : start + count, :] = jnp.where(core_ref[0] == 0, mine, theirs)
        out_ref[start + count : start + 2 * count, :] = jnp.where(core_ref[0] == 0, theirs, mine)
        out_ref[start + 2 * count : start + room, :] = jnp.zeros(
            (room - 2 * count, out_ref.shape[1]), out_ref.dtype
        )
        start += room


def join_gate_up(flags_ref, shared_ref, shared_other, expert_ref, expert_other, extra_ref, out_ref):
    chips, rows, shared_wide = shared_ref.shape
    core = flags_ref[0]
    for chip in range(chips):
        mine = shared_ref[chip]
        theirs = shared_other[chip]
        start = 2 * rows * chip
        out_ref[start : start + rows, :shared_wide] = jnp.where(core == 0, mine, theirs)
        out_ref[start + rows : start + 2 * rows, :shared_wide] = jnp.where(core == 0, theirs, mine)
    blocks = 512 // out_ref.shape[0]
    row_core = (pl.program_id(0) // blocks) & 1
    expert = jnp.where(row_core == core, expert_ref[0], expert_other[0])
    half = expert.shape[1] // 2
    out_ref[:, shared_wide:] = expert
    last = expert[:, half - 128 : half]
    out_ref[:, shared_wide + half - 128 : shared_wide + half] = last + extra_ref[...]


def assemble(flags, shared, shared_other, expert, expert_other, extra):
    chips, depth, shared_wide = shared.shape
    expert_wide = expert.shape[2]
    width = 2 * chips * depth
    block = 256
    per = block // (2 * depth)
    blocks = expert.shape[1] // block

    def expert_block(b, flags):
        return ((b // (2 * blocks)) ^ flags[1], b % blocks, 0)

    shared_spec = pl.BlockSpec((per, depth, shared_wide), lambda b, flags: (b, 0, 0))
    expert_spec = pl.BlockSpec((1, block, expert_wide), expert_block)
    wide = shared_wide + expert_wide
    return pl.pallas_call(
        join_gate_up,
        grid_spec=pltpu.PrefetchScalarGridSpec(
            num_scalar_prefetch=1,
            grid=(width // block,),
            in_specs=[
                shared_spec,
                shared_spec,
                expert_spec,
                expert_spec,
                pl.BlockSpec((block, 128), lambda b, flags: (b, 0)),
            ],
            out_specs=pl.BlockSpec((block, wide), lambda b, flags: (b, 0)),
        ),
        out_shape=shape_of((width, wide)),
        cost_estimate=pl.CostEstimate(
            flops=0, bytes_accessed=6 * width * wide, transcendentals=0
        ),
        compiler_params=pltpu.CompilerParams(vmem_limit_bytes=40 * 1024 * 1024),
    )(flags, shared, shared_other, expert, expert_other, extra)


def expert_kernel(
    sizes,
    expert_ref,
    rows_ref,
    branch_ref,
    mask_ref,
    gate_up_ref,
    down_ref,
    hidden_ref,
    grad_ref,
    out_ref,
    back_out,
    joined,
    back,
):
    shared_wide, expert_wide, tail_lane, experts = sizes
    padded = shared_wide + expert_wide
    joined[...] = mm(rows_ref[...], gate_up_ref[...])
    back[...] = mm_nt(branch_ref[...], down_ref[...])

    tail_at = 2 * shared_wide + expert_wide - 128
    logits = joined[:, tail_at : tail_at + 128]
    lane = lax.broadcasted_iota(jnp.int32, logits.shape, 1)
    routed = (lane >= tail_lane) & (lane < tail_lane + experts)
    top = jnp.max(jnp.where(routed, logits, negative), axis=1, keepdims=True)
    powers = jnp.where(routed, jnp.exp(jnp.where(routed, logits - top, 0.0)), 0.0)
    router_probs = powers / jnp.sum(powers, axis=1, keepdims=True)
    one_expert = lane == tail_lane + expert_ref[0]
    my_prob = jnp.sum(jnp.where(one_expert, router_probs, 0.0), axis=1, keepdims=True)
    is_gate = lane == tail_lane + experts
    gate_logit = jnp.sum(jnp.where(is_gate, logits, 0.0), axis=1, keepdims=True)
    shared_weight = jax.nn.sigmoid(gate_logit)
    mask = mask_ref[...]
    alongs = []
    at = 0
    for wide, weight in ((shared_wide, shared_weight), (expert_wide, my_prob * mask)):
        along = jnp.zeros_like(my_prob)
        for start in range(0, wide, 128):
            gate_at = 2 * at + start
            gate = joined[:, gate_at : gate_at + 128]
            up = joined[:, gate_at + wide : gate_at + wide + 128]
            back_part = back[:, at + start : at + start + 128]
            sigmoid_gate = jax.nn.sigmoid(gate)
            silu = gate * sigmoid_gate
            hidden = silu * up
            hidden_ref[:, at + start : at + start + 128] = (hidden * weight).astype(BF16)
            along = along + jnp.sum(hidden * back_part, axis=1, keepdims=True)
            grad_hidden = back_part * weight
            gate_grad = grad_hidden * up * sigmoid_gate * (1.0 + gate * (1.0 - sigmoid_gate))
            grad_ref[:, gate_at + wide : gate_at + wide + 128] = (grad_hidden * silu).astype(BF16)
            if gate_at != tail_at:
                grad_ref[:, gate_at : gate_at + 128] = gate_grad.astype(BF16)
            else:
                tail_grad = gate_grad
        alongs.append(along)
        at += wide
    logit_grad = router_probs * (alongs[1] * mask) * (jnp.where(one_expert, 1.0, 0.0) - my_prob)
    shared_logit_grad = alongs[0] * shared_weight * (1.0 - shared_weight)
    tail_grad = tail_grad + jnp.where(is_gate, shared_logit_grad, logit_grad)
    grad_ref[:, tail_at : tail_at + 128] = tail_grad.astype(BF16)

    out_ref[...] = mm(hidden_ref[...], down_ref[...]).astype(BF16)
    back_out[...] = mm_nt(grad_ref[...], gate_up_ref[...]).astype(BF16)


def relative_kernel(places_ref, in_ref, out_ref, sems):
    group = in_ref.shape[0]
    chips = pl.num_programs(0) * group
    copies = []
    start = 0
    from_row = 0
    for number, count in enumerate(SPLITS):
        for own in range(group):
            place = places_ref[number * chips + pl.program_id(0) * group + own]
            copies.append(
                pltpu.make_async_copy(
                    in_ref.at[own, pl.ds(from_row, count), :],
                    out_ref.at[pl.ds(pl.multiple_of(start + place * count, 8), count), :],
                    sems.at[number * group + own],
                )
            )
        start += chips * count
        from_row += count
    for copy in copies:
        copy.start()
    for copy in copies:
        copy.wait()


def to_relative(places, value):
    chips, rows, width = value.shape
    group = 4
    return pl.pallas_call(
        relative_kernel,
        grid=(chips // group,),
        out_shape=shape_of((chips * rows, width)),
        in_specs=[
            pl.BlockSpec(memory_space=pltpu.SMEM),
            pl.BlockSpec((group, rows, width), lambda c: (c, 0, 0)),
        ],
        out_specs=pl.BlockSpec(memory_space=pl.ANY),
        scratch_shapes=[pltpu.SemaphoreType.DMA((len(SPLITS) * group,))],
        cost_estimate=pl.CostEstimate(
            flops=0, bytes_accessed=4 * chips * rows * width, transcendentals=0
        ),
    )(places, value)


def expert_pass(sizes, my_expert, rows, branch, mask, gate_up, down):
    shared_wide, expert_wide, _, _ = sizes
    padded = shared_wide + expert_wide
    count, width = rows.shape
    tile = 256
    once = dict(pipeline_mode=pl.Buffered(1))

    def at(i):
        return (i, 0)

    def fixed(i):
        return (0, 0)

    return pl.pallas_call(
        lambda *refs: expert_kernel(sizes, *refs),
        grid=(count // tile,),
        in_specs=[
            pl.BlockSpec(memory_space=pltpu.SMEM),
            pl.BlockSpec((tile, width), at),
            pl.BlockSpec((tile, width), at),
            pl.BlockSpec((tile, 1), at),
            pl.BlockSpec((width, 2 * padded), fixed, **once),
            pl.BlockSpec((padded, width), fixed, **once),
        ],
        out_specs=[
            pl.BlockSpec((tile, padded), at),
            pl.BlockSpec((tile, 2 * padded), at),
            pl.BlockSpec((tile, width), at),
            pl.BlockSpec((tile, width), at),
        ],
        out_shape=[
            shape_of((count, padded)),
            shape_of((count, 2 * padded)),
            shape_of((count, width)),
            shape_of((count, width)),
        ],
        scratch_shapes=[pltpu.VMEM((tile, 2 * padded), F32), pltpu.VMEM((tile, padded), F32)],
        cost_estimate=pl.CostEstimate(
            flops=count * width * padded,
            bytes_accessed=8 * count * width,
            transcendentals=0,
        ),
        compiler_params=pltpu.CompilerParams(vmem_limit_bytes=58 * 1024 * 1024),
    )(my_expert.reshape(1), rows, branch, mask, gate_up, down)


def rotary_tables(positions):
    freq_index = jnp.arange(HEAD // 2).astype(F32)
    inverse = jnp.exp(freq_index * (-2.0 * math.log(rope_base) / HEAD))
    angles = positions.astype(F32)[:, None] * inverse[None, :]
    cosine = jnp.concatenate([jnp.cos(angles), jnp.cos(angles)], axis=-1)
    sine_table = jnp.concatenate([jnp.sin(angles), jnp.sin(angles)], axis=-1)
    return (cosine, sine_table)


def rotate(values, cosine, sine_table):
    half_width = HEAD // 2
    turned = jnp.concatenate([-values[..., half_width:], values[..., :half_width]], axis=-1)
    return values * cosine + turned * sine_table


def rotate_back(grads_in, cosine, sine_table):
    half_width = HEAD // 2
    scaled = grads_in * sine_table
    turned = jnp.concatenate([scaled[..., half_width:], -scaled[..., :half_width]], axis=-1)
    return grads_in * cosine + turned


def normalize(values):
    factor = lax.rsqrt(jnp.mean(values * values, axis=-1, keepdims=True) + epsilon)
    return (values * factor, factor)


def norm_back(grad_normed, normal, factor, gain_vector):
    scaled = grad_normed * gain_vector
    grad_input = factor * (scaled - normal * jnp.mean(scaled * normal, axis=-1, keepdims=True))
    return (grad_input, jnp.sum(grad_normed * normal, axis=0))


def on_device(
    tokens,
    cotangent,
    lengths,
    order,
    routes,
    norm_attn,
    q_weight,
    k_weight,
    v_weight,
    q_bias,
    k_bias,
    v_bias,
    o_weight,
    norm_moe,
    router,
    shared_gate,
    shared_gate_up,
    shared_down,
    expert_gate_up,
    expert_down,
):
    total = devices()
    chips = total // 2
    bit_count = total.bit_length() - 1
    high = tuple(range(4, bit_count))
    me = lax.axis_index(AXES)
    core = me & 1
    x_bit = (me >> 1) & 1
    pair = (me >> 1) & 7
    upper = me >> 4
    uppers = total // 16
    parts = 2 * uppers
    part = upper * 2 + core
    my_expert = me >> 2
    sequences, piece, width = tokens.shape
    experts = router.shape[1]
    rows = sequences * piece
    length = total * piece
    own_seq = sequences // parts
    depth = q_weight.shape[0]
    heads = width // HEAD
    shared_width = shared_down.shape[0] * total // chips
    expert_width = expert_down.shape[1] * 2
    shared_wide = -(-shared_width // 128) * 128
    expert_wide = -(-(expert_width + experts + 1) // 128) * 128
    padded = shared_wide + expert_wide
    tail_at = 2 * shared_wide + expert_width
    groups = total // 4
    per_group = sequences // groups
    group_rows = per_group * groups * piece
    capacity = (5 * group_rows * TOP + 4 * experts - 1) // (4 * experts)
    score_scale = HEAD ** (-0.5)
    low_orders = rotations(())

    small = jnp.concatenate(
        [
            jnp.stack([norm_attn, q_bias, k_bias, v_bias, norm_moe, shared_gate]),
            router.T,
            jnp.zeros((2, depth), BF16),
        ]
    )
    dealt_tokens, tokens_arrived = deal(tokens, part, high)
    small = after(small, *tokens_arrived)
    small = jnp.broadcast_to(small[None], (total,) + small.shape)
    small = lax.all_to_all(small, AXES, split_axis=0, concat_axis=0, tiled=True)
    small = small.transpose(1, 0, 2).reshape(small.shape[1], width)
    gain_attn = small[0].astype(F32)
    gain_moe = small[4].astype(F32)
    biases = lax.dynamic_slice_in_dim(small[1:4].reshape(3, heads // 2, 2, HEAD), pair, 1, axis=1)
    biases = biases[:, 0].transpose(1, 0, 2).astype(F32)

    token_parts = gather_parts(pieces(dealt_tokens.reshape(rows, width)), low_orders)

    by_head = whole_kernel(
        split_heads, [shape_of((total, depth, 3 * HEAD))], q_weight, k_weight, v_weight
    )[0]
    my_head = lax.all_to_all(
        by_head, AXES, split_axis=0, concat_axis=0, tiled=True
    ).reshape(width, 3 * HEAD)
    other_head = swap(my_head, 0)
    qkv_weight = jnp.concatenate(
        [
            jnp.where(core == 0, my_head, other_head),
            jnp.where(core == 0, other_head, my_head),
        ],
        axis=1,
    )

    o_places = []
    for k in range(uppers):
        o_places.append(
            [
                (
                    i,
                    (((i % parts >> 1) ^ k) << 4) | ((i // parts) << 1) | (i & 1),
                )
                for i in range(total)
            ]
        )
    o_rows = xor_order(jnp.stack([permute(o_weight, places) for places in o_places]), upper)
    o_rows = by_bit(o_rows, swap(o_rows, 0), core, 1).reshape(2 * HEAD, width)

    own_positions = me * piece + jnp.arange(piece, dtype=jnp.int32)
    live_own = (own_positions[None, :] < lengths[:, None]).astype(F32)[:, :, None]
    grad_out = cotangent.astype(F32)
    branch_own = (live_own * grad_out).astype(BF16).reshape(rows, width)
    branch_all = lax.all_gather(after(branch_own, *token_parts), CHIPS, axis=0)
    chip_number = jnp.arange(chips, dtype=jnp.int32) ^ (me >> 1)
    chip_places = []
    for order_of in rotations(()):
        place_of_chip = np.zeros((chips,), np.int32)
        place_of_chip[relative(rest_of(high, order_of)) >> 1] = np.arange(chips)
        chip_places.append(jnp.take(jnp.asarray(place_of_chip), chip_number))
    branch = to_relative(jnp.concatenate(chip_places), branch_all)

    shared_pieces = whole_kernel(
        split_columns, [shape_of((chips, depth, 2 * shared_wide))], shared_gate_up
    )[0]
    shared_pieces = after(shared_pieces, *token_parts)
    shared_in = lax.all_to_all(shared_pieces, CHIPS, split_axis=0, concat_axis=0, tiled=True)
    shared_other = swap(shared_in, 0)
    expert_rows = expert_gate_up.shape[1]
    expert_halves = whole_kernel(
        split_columns, [shape_of((2, expert_rows, 2 * expert_wide))], expert_gate_up[0]
    )[0]
    keep_half = lax.dynamic_index_in_dim(expert_halves, x_bit, 0, keepdims=False)
    give_half = lax.dynamic_index_in_dim(expert_halves, 1 - x_bit, 0, keepdims=False)
    give_half = after(give_half, *token_parts)
    expert_got = swap(give_half, 1)
    expert_in = jnp.stack([keep_half, expert_got])
    expert_other = swap(expert_in, 0)
    extra = jnp.concatenate(
        [
            jnp.zeros((expert_width - expert_wide + 128, width), BF16),
            small[6 : 6 + experts],
            small[5:6],
            jnp.zeros((expert_wide - expert_width - experts - 1, width), BF16),
        ]
    ).T
    gate_up_weight = assemble(
        jnp.stack([core, x_bit]), shared_in, shared_other, expert_in, expert_other, extra
    )
    down_weight = whole_kernel(
        join_down,
        [shape_of((padded, width))],
        core.reshape(1),
        shared_down,
        swap(shared_down, 0),
        expert_down[0],
        swap(expert_down[0], 0),
    )[0]

    all_positions = jnp.arange(length, dtype=jnp.int32)
    named = jnp.any(routes == my_expert, axis=-1) & (all_positions[None, :] < lengths[:, None])
    dealt = (
        jnp.take(named, order, axis=0)
        .reshape(groups, per_group, length // (4 * piece), 4, piece)
        .transpose(0, 3, 1, 2, 4)
        .reshape(groups * 4, group_rows)
        .astype(BF16)
    )
    index = jnp.arange(group_rows, dtype=jnp.int32)
    before = mm(dealt, (index[:, None] < index[None, :]).astype(BF16))
    kept = (
        jnp.where(before < capacity, dealt.astype(F32), 0.0)
        .reshape(groups, 4, per_group, length // (4 * piece), piece)
        .transpose(0, 2, 3, 1, 4)
        .reshape(sequences, length)
    )
    seq_index = jnp.arange(sequences, dtype=jnp.int32)
    place_of = jnp.sum(
        jnp.where(order[None, :] == seq_index[:, None], seq_index[None, :], 0), axis=1
    )
    kept = (
        jnp.take(kept, place_of, axis=0)
        .reshape(sequences, total, piece)
        .transpose(1, 0, 2)
        .reshape(total, rows)
    )

    wanted = (3, 2, 1)
    normed_parts = []
    projected = []
    for value, bits in zip(token_parts, low_orders, strict=True):
        flat = value.reshape(-1, width).astype(F32)
        normed = (normalize(flat)[0] * gain_attn).astype(BF16)
        normed_parts.append(normed)
        out = mm(normed, qkv_weight).reshape(value.shape[:-1] + (6 * HEAD,))
        projected.append(to_order(out, bits, wanted))
    shape_rows = (8, parts, own_seq, piece, 2, 3, HEAD)
    joined = jnp.concatenate(projected, axis=-2).reshape(shape_rows)
    joined = joined + biases
    joined = joined.transpose(5, 2, 4, 0, 1, 3, 6).reshape(3, own_seq, 2, length, HEAD)
    source = relative(tuple(reversed(high)) + (0,))
    low_relative = relative(LOW)
    rel = (low_relative[:, None] ^ source[None, :]).reshape(-1)
    positions = (
        (me ^ jnp.asarray(rel, jnp.int32))[:, None] * piece
        + jnp.arange(piece, dtype=jnp.int32)[None, :]
    ).reshape(-1)
    causal = positions[None, :] <= positions[:, None]
    cosine, sine_table = rotary_tables(positions)
    queries = rotate(joined[0], cosine, sine_table).astype(BF16)
    keys = rotate(joined[1], cosine, sine_table).astype(BF16)
    values = joined[2].astype(BF16)
    scores = (
        jnp.einsum("shqd,shkd->shqk", queries, keys, preferred_element_type=F32) * score_scale
    )
    masked = jnp.where(causal[None, None], scores, negative)
    top_score = jnp.max(masked, axis=-1, keepdims=True)
    log_total = top_score + jnp.log(jnp.sum(jnp.exp(masked - top_score), axis=-1, keepdims=True))
    probs = jnp.exp(masked - log_total).astype(BF16)
    attended = jnp.einsum("shqk,shkd->shqd", probs, values, preferred_element_type=F32)

    def to_parts(value):
        columns = value.shape[0]
        value = value.reshape(columns, own_seq, 2, 8, parts, piece, HEAD)
        value = value.transpose(3, 4, 1, 5, 2, 0, 6).reshape(2, 2, 2, rows, 2 * columns * HEAD)
        return [
            to_order(part_rows, (1, 2, 3), tuple(reversed(bits))).reshape(
                8 * part_rows.shape[-2], -1
            )
            for part_rows, bits in zip(pieces(value), low_orders, strict=True)
        ]

    def reduce_low(parts_in):
        found = [value.astype(BF16).reshape(2, 2, 2, -1, width) for value in parts_in]
        for step in range(len(LOW)):
            got = [
                swap(value[1], bits[-1 - step])
                for value, bits in zip(found, low_orders, strict=True)
            ]
            keeps, got = together([value[0] for value in found], got)
            found = [add_low(keep, other) for keep, other in zip(keeps, got, strict=True)]
        found = jnp.concatenate(found).reshape(
            (2,) * (1 + len(high)) + (own_seq, piece, width)
        )
        return found

    attended_parts = to_parts(attended.astype(BF16)[None])
    attended_parts[0] = after(attended_parts[0], shared_in, expert_got)
    attn_out = reduce_low([mm(value, o_rows) for value in attended_parts])
    attn_out = undeal(attn_out, part, high)
    attn_out = after(attn_out, branch_all)
    inputs = tokens.astype(F32)
    residual = (inputs + live_own * attn_out.astype(F32)).reshape(rows, width)
    normal_two, factor_two = normalize(residual)
    normed_own = (normal_two * gain_moe).astype(BF16)

    expert_column = jnp.arange(experts, dtype=jnp.int32)[None, :]
    one_expert = (expert_column == my_expert).astype(F32)
    everyone = Gather(normed_own, high)
    everyone.value = after(everyone.value, gate_up_weight, down_weight, branch)
    everyone.split()
    for _ in LOW:
        everyone.step()
    everyone = everyone.whole()
    masks = []
    start = 0
    for count, order_of in zip(SPLITS, rotations(()), strict=True):
        places = me ^ jnp.asarray(relative(rest_of(high, order_of)), jnp.int32)
        masks.append(jnp.take(kept[:, start : start + count], places, axis=0).reshape(-1, 1))
        start += count

    sizes = (shared_wide, expert_wide, expert_width - expert_wide + 128, experts)

    hidden, joined_grad, out_rows, back_rows = expert_pass(
        sizes, my_expert, everyone, branch, jnp.concatenate(masks), gate_up_weight, down_weight
    )
    grad_sum = Reduction(back_rows, high, chips)
    out_sum = Reduction(out_rows, high, chips)
    grad_sum.send()
    grad_gate_up = mm_tn(everyone, joined_grad).astype(BF16)
    grad_sum.add()
    grad_sum.send(grad_gate_up)
    grad_down = mm_tn(after(hidden, grad_gate_up), branch).astype(BF16)
    grad_sum.add()
    grad_sum.send(grad_down)
    grad_sum.add()
    grad_parts = [grad_sum.finish()]
    live_rows = jnp.broadcast_to(live_own, (sequences, piece, 1)).reshape(rows, 1)
    grad_normed = grad_parts[0].astype(F32)
    grad_residual_in, grad_gain_moe = norm_back(grad_normed, normal_two, factor_two, gain_moe)
    grad_residual = grad_out.reshape(rows, width) + grad_residual_in

    attn_grad = (live_rows * grad_residual).astype(BF16).reshape(tokens.shape)
    dealt_grad, grad_arrived = deal(attn_grad, part, high)
    attn_grad_parts = gather_parts(pieces(dealt_grad.reshape(rows, width)), low_orders)
    out_sum.send(*attn_grad_parts)
    attended_grads = []
    grad_o = 0.0
    for value, ahead, bits in zip(attn_grad_parts, attended_parts, low_orders, strict=True):
        flat = value.reshape(-1, width)
        back = mm_nt(flat, o_rows).astype(BF16).reshape(value.shape[:-1] + (2 * HEAD,))
        attended_grads.append(to_order(back, bits, wanted))
        grad_o = grad_o + mm_tn(ahead, flat)
    def pick(value, axis, number):
        return lax.dynamic_index_in_dim(value, number, axis, keepdims=False)

    def to_core(value, axis):
        given_rows = swap(pick(value, axis, 1 - core), 0)
        return pick(value, axis, core).astype(F32) + given_rows.astype(F32)

    def to_owners(vectors):
        vectors = vectors.reshape(-1, total, depth).transpose(1, 0, 2)
        vectors = lax.all_to_all(vectors, AXES, split_axis=0, concat_axis=0, tiled=True)
        return jnp.sum(vectors, axis=0)

    grad_gate_up, grad_down = after((grad_gate_up, grad_down), *grad_arrived)
    tail_grads = grad_gate_up[:, tail_at : tail_at + experts + 1].astype(F32)
    grad_shared_gu = to_core(
        grad_gate_up[:, : 2 * shared_wide].reshape(chips, 2, depth, 2 * shared_wide), 1
    ).astype(BF16)
    grad_expert_gu = to_core(
        grad_gate_up[:, 2 * shared_wide :].reshape(2, 2, expert_rows, 2 * expert_wide), 1
    ).astype(BF16)
    grad_shared_down = to_core(grad_down[:shared_width].reshape(2, -1, width), 0)
    grad_expert_down = to_core(
        grad_down[shared_wide : shared_wide + expert_width].reshape(2, -1, width), 0
    )
    vectors = to_owners(jnp.concatenate([grad_gain_moe[None], tail_grads.T], axis=0))
    attended_grad = after(
        jnp.concatenate(attended_grads, axis=-2), grad_shared_gu, grad_expert_gu
    )
    grad_shared_gu, grad_expert_gu = after((grad_shared_gu, grad_expert_gu), *attn_grad_parts)
    grad_shared_gu = lax.all_to_all(
        grad_shared_gu, CHIPS, split_axis=0, concat_axis=0, tiled=True
    )
    mine_gu = pick(grad_expert_gu, 0, x_bit)
    theirs_gu = swap(pick(grad_expert_gu, 0, 1 - x_bit), 1)
    grad_o = to_core(grad_o.astype(BF16).reshape(uppers, 2, depth, width), 1).astype(BF16)
    grad_o = xor_order(grad_o, upper)
    attended_grad = (
        attended_grad.reshape(8, parts, own_seq, piece, 2, HEAD)
        .transpose(2, 4, 0, 1, 3, 5)
        .reshape(own_seq, 2, length, HEAD)
    )
    again = jnp.exp(masked - log_total)
    prob_grad = jnp.einsum("shqd,shkd->shqk", attended_grad, values, preferred_element_type=F32)
    inner_sum = jnp.sum(again * prob_grad, axis=-1, keepdims=True)
    score_grad = (again * (prob_grad - inner_sum)).astype(BF16)
    grad_query = (
        jnp.einsum("shqk,shkd->shqd", score_grad, keys, preferred_element_type=F32) * score_scale
    )
    grad_key = (
        jnp.einsum("shqk,shqd->shkd", score_grad, queries, preferred_element_type=F32)
        * score_scale
    )
    grad_value = jnp.einsum("shqk,shqd->shkd", probs, attended_grad, preferred_element_type=F32)
    grads = jnp.stack(
        [
            rotate_back(grad_query, cosine, sine_table).astype(BF16),
            rotate_back(grad_key, cosine, sine_table).astype(BF16),
            grad_value.astype(BF16),
        ]
    )
    out_waits = list(out_sum.got)
    out_sum.add()
    grads = after(grads, vectors, *out_waits)
    out_sum.send()
    bias_grads = jnp.sum(grads.astype(F32), axis=(1, 3))
    grads_parts = to_parts(grads)
    grad_qkv = 0.0
    for value, normed in zip(grads_parts, normed_parts, strict=True):
        grad_qkv = grad_qkv + mm_tn(normed, value)
    grad_qkv = grad_qkv.astype(BF16)
    low_head = grad_qkv[:, : 3 * HEAD]
    high_head = grad_qkv[:, 3 * HEAD :]
    give_head = jnp.where(core == 0, high_head, low_head)
    out_waits = list(out_sum.got)
    out_sum.add()
    given_head = swap(give_head, 0)
    grads_parts[0] = after(grads_parts[0], given_head, *out_waits)
    out_sum.send()
    keep_head = jnp.where(core == 0, low_head, high_head)
    grad_qkv = lax.all_to_all(
        add_low(keep_head, given_head).reshape(total, depth, 3 * HEAD),
        AXES,
        split_axis=0,
        concat_axis=0,
        tiled=True,
    )
    normed_sum = [
        mm_nt(value, qkv_weight).astype(BF16).reshape(2, 2, 2, -1, width) for value in grads_parts
    ]
    for step in range(len(LOW)):
        got = [
            swap(value[1], order_of[-1 - step])
            for value, order_of in zip(normed_sum, low_orders, strict=True)
        ]
        waits = list(got)
        if step == 0:
            waits += [grad_shared_gu, theirs_gu, *out_sum.got]
            out_sum.add()
        if step == 1:
            waits += [grad_qkv]
        keeps, got = together([value[0] for value in normed_sum], after(tuple(got), *waits[3:]))
        normed_sum = [add_low(keep, other) for keep, other in zip(keeps, got, strict=True)]
    moe_out = out_sum.finish().astype(F32)
    grad_o = after(grad_o, *got)
    grad_o = sum(
        permute(grad_o[k], [(b, a) for a, b in places]).astype(F32)
        for k, places in enumerate(o_places)
    )
    grad_normed_one = jnp.concatenate(normed_sum).reshape(dealt_grad.shape)
    grad_normed_one = undeal(grad_normed_one, part, high).astype(F32).reshape(rows, width)
    grad_qkv = whole_kernel(join_heads, [shape_of((depth, width), F32)] * 3, grad_qkv)
    grad_shared_gu = whole_kernel(
        join_columns, [shape_of((depth, 2 * chips * shared_width), F32)], grad_shared_gu
    )[0]
    grad_expert_gu = whole_kernel(
        join_halves,
        [shape_of((expert_rows, 4 * expert_width), F32)],
        x_bit.reshape(1),
        mine_gu,
        theirs_gu,
    )[0][None]
    normal_one, factor_one = normalize(inputs.reshape(rows, width))
    grad_input, grad_gain_attn = norm_back(grad_normed_one, normal_one, factor_one, gain_attn)
    grad_tokens = (grad_residual + grad_input).astype(BF16).reshape(tokens.shape)
    mixed = (residual + live_rows * moe_out).astype(BF16).reshape(tokens.shape)

    bias_rows = lax.dynamic_update_slice_in_dim(
        jnp.zeros((3, heads // 2, 2 * HEAD), F32),
        bias_grads.reshape(3, 1, 2 * HEAD),
        pair,
        axis=1,
    ).reshape(3, width)
    ends = to_owners(jnp.concatenate([bias_rows, grad_gain_attn[None]], axis=0))
    return (
        mixed,
        grad_tokens,
        ends[3],
        grad_qkv[0],
        grad_qkv[1],
        grad_qkv[2],
        ends[0],
        ends[1],
        ends[2],
        grad_o,
        vectors[0],
        vectors[1 : 1 + experts].T,
        vectors[1 + experts],
        grad_shared_gu,
        grad_shared_down,
        grad_expert_gu,
        grad_expert_down[None],
    )


def solution(mesh):
    fine = Mesh(mesh.devices.reshape(mesh.devices.size // 4, 2, 2), AXES)
    given = P(None, AXES, None)
    rows = P(AXES, None)
    vector = P(AXES)
    expert = P("dp", ("x", "core"), None)
    in_specs = (
        given,
        given,
        P(),
        P(),
        P(),
        vector,
        rows,
        rows,
        rows,
        vector,
        vector,
        vector,
        rows,
        vector,
        rows,
        vector,
        rows,
        rows,
        expert,
        expert,
    )
    out_specs = (
        given,
        given,
        vector,
        rows,
        rows,
        rows,
        vector,
        vector,
        vector,
        rows,
        vector,
        rows,
        vector,
        rows,
        rows,
        expert,
        expert,
    )
    return jax.shard_map(
        on_device, mesh=fine, in_specs=in_specs, out_specs=out_specs, check_vma=False
    )
```
